512 devices in a mesh: leaf: 256 (over z, y, x), blk: 2 (over core).
Axes of the slice: x: 4, y: 4, z: 16, core: 2. Of those that a mesh axis runs over, the one named last changes fastest.
Arguments:
- obs_rows: bfloat16 [131072, 512], P('leaf'), may hold values from -0.25 to 0.25
- obs_values: float32 [131072], P('leaf'), may hold values from -24 to 24
- track_blocks: int32 [256], P('leaf'), may hold values from 1 to 4, as said below
- pattern: int32 [1024, 64], P('leaf'), may hold values 0 or 1
- process_info: float32 [512, 512], replicated, as said below
Outputs:
- leaf_mean: float32 [256, 512], P('leaf')
- leaf_cov: float32 [131072, 512], P('leaf', 'blk')
The draws below stay inside these ranges and needn't reach their ends.
Inputs may be any that keep to these rules, and one draw needn't show every extreme that they name: `track_blocks`: some leaf has exactly 4 live row blocks in every draw; the others have 1 to 3. `process_info`: symmetric positive definite.
All inputs are finite; a program needn't handle non-finite values. No bound on the sum of `pattern` on one device may be relied on, other than what follows from the above.
Results may differ from the reference program's by a relative error of at most 0.0003.
Values sent between devices are 32-bit elements; how exact they have to be, the bound alone decides.
A program may use at most 128 MiB of HBM per device.

```python
import jax
import jax.numpy as jnp
from jax import lax

S = 512
PATBLK = 64
CAPB = 4
LEAVES = 256
ROWS = 512


def draw_track_blocks(key, part):
    first_key, second_key = jax.random.split(key)
    base_counts = jax.random.randint(first_key, (LEAVES,), 1, CAPB // 2 + 2)
    base_counts = jnp.minimum(base_counts, CAPB)
    busiest = jax.random.randint(second_key, (), 0, LEAVES)
    return jnp.where(jnp.arange(LEAVES) == busiest, CAPB, base_counts).astype(jnp.int32)


def draw_process_info(key, part):
    first_key, second_key = jax.random.split(jax.random.fold_in(key, 7))
    mixing = jax.random.normal(first_key, (S, S), jnp.float32)
    diagonal = jax.random.uniform(second_key, (S,), jnp.float32, 1.0, 2.0)
    square = jnp.dot(mixing, mixing.T, precision=lax.Precision.HIGHEST) / S
    square = 0.5 * (square + square.T)
    return 0.5 * (square + jnp.diag(diagonal))


def set_ends(array, key, smallest, largest):
    index_at = [jax.random.randint(jax.random.fold_in(key, axis), (), 0, length) for axis, length in enumerate(array.shape)]
    longest = array.shape.index(max(array.shape))
    beside = index_at[:longest] + [(index_at[longest] + 1) % array.shape[longest]] + index_at[longest + 1:]
    return array.at[tuple(index_at)].set(smallest).at[tuple(beside)].set(largest)


def shard_levels(own_key, extent, shards, low, largest):
    def one(position, blocks):
        steps = jax.random.uniform(jax.random.fold_in(jax.random.fold_in(own_key, 6), position), (blocks,), jnp.float32, low / len(shards), largest / len(shards))
        return jnp.repeat(jnp.exp(steps), extent[position] // blocks).reshape((-1,) + (1,) * (len(extent) - position - 1))

    loudness = one(*shards[0])
    for cut in shards[1:]:
        loudness = loudness * one(*cut)
    return loudness


def scatter_about(rng, shape, spread, limit, cuts=(), held_as=jnp.bfloat16):
    level = shard_levels(rng, shape, cuts, -0.22, 0.18) if cuts else 1.0
    array = jax.random.normal(rng, shape, jnp.float32) * spread * level
    return jnp.minimum(jnp.maximum(array, -limit), limit).astype(held_as)


def setup_inputs(seed: int = 0) -> dict:
    streams_of = jax.random.split(jax.random.key(seed), 6)
    return {
        "obs_rows": scatter_about(streams_of[0], (LEAVES * ROWS, S), S ** -0.5, 0.25, ((0, 256),)),
        "obs_values": scatter_about(streams_of[1], (LEAVES * ROWS,), 4.0, 24.0, ((0, 256),), jnp.float32),
        "track_blocks": draw_track_blocks(jax.random.fold_in(streams_of[5], 71), 0),
        "pattern": set_ends((jax.random.randint(streams_of[3], (LEAVES * CAPB, PATBLK), 0, 2) < 1).astype(jnp.int32), jax.random.fold_in(streams_of[3], 1), 0, 1),
        "process_info": draw_process_info(jax.random.fold_in(streams_of[5], 71), 0),
    }


highest = lax.Precision.HIGHEST

def product(left, right):
    return jnp.dot(left.astype(jnp.float32), right.astype(jnp.float32), precision=highest, preferred_element_type=jnp.float32)

def solve(factor, right):
    return jax.scipy.linalg.cho_solve((factor, True), right)

def reference(obs_rows, obs_values, track_blocks, pattern, process_info):
    leaves = track_blocks.shape[0]
    levels = (leaves.bit_length() - 1) // 2
    states = process_info.shape[0]
    cap_blocks = pattern.shape[0] // leaves
    block_width = states // pattern.shape[1]
    keep_mask = jnp.repeat(pattern.astype(jnp.bfloat16), block_width, axis=1).reshape(leaves, cap_blocks, states)
    alive_mask = (jnp.arange(cap_blocks)[None, :] < track_blocks[:, None]).astype(jnp.bfloat16)
    keep_mask = keep_mask * alive_mask[:, :, None]
    masked_rows = obs_rows.reshape(leaves, cap_blocks, -1, states) * keep_mask[:, :, None, :]
    masked_rows = masked_rows.reshape(leaves, -1, states)
    values = obs_values.reshape(leaves, -1)

    def leaf_info(item):
        flat_rows, leaf_values = item
        gram = jnp.dot(flat_rows.T.astype(jnp.float32), flat_rows.astype(jnp.float32), preferred_element_type=jnp.float32)
        vector = jnp.dot(leaf_values.astype(jnp.float32), flat_rows.astype(jnp.float32), precision=highest, preferred_element_type=jnp.float32)
        return (gram, vector)
    info, vecs = lax.map(leaf_info, (masked_rows, values))

    def node_up(item):
        node_info, node_vec = item
        factor = jnp.linalg.cholesky(node_info + process_info)
        gain = solve(factor, process_info)
        msg_info = process_info - product(process_info, gain)
        msg_vec = product(process_info, solve(factor, node_vec))
        return (factor, gain, msg_info, msg_vec)
    stored = []
    for tier_index in range(levels):
        factor, gain, msg_info, msg_vec = lax.map(node_up, (info, vecs))
        stored.append((factor, gain, vecs))
        count = msg_info.shape[0] // 4
        info = msg_info.reshape(count, 4, states, states).sum(axis=1)
        vecs = msg_vec.reshape(count, 4, states).sum(axis=1)
    root_factor = jnp.linalg.cholesky(info[0] + process_info)
    identity = jnp.eye(states, dtype=jnp.float32)
    means = solve(root_factor, vecs[0])[None, :]
    covs = solve(root_factor, identity)[None]

    def node_down(item):
        node_factor, node_gain, node_vec, mean_up, cov_up = item
        inner_prod = lax.dot_general(cov_up.astype(jnp.float32), node_gain.astype(jnp.float32), (((1,), (1,)), ((), ())), precision=highest, preferred_element_type=jnp.float32)
        cov_node = solve(node_factor, identity + product(process_info, inner_prod))
        mean_node = solve(node_factor, node_vec + product(process_info, mean_up))
        return (mean_node, cov_node)
    for tier_index in range(levels - 1, -1, -1):
        factor, gain, node_vecs = stored[tier_index]
        parent_means = jnp.repeat(means, 4, axis=0)
        parent_covs = jnp.repeat(covs, 4, axis=0)
        means, covs = lax.map(node_down, (factor, gain, node_vecs, parent_means, parent_covs))
    return (means, covs.reshape(leaves * states, states))
```

```python
import functools

import jax
import jax.numpy as jnp
from jax import lax
from jax.experimental import pallas as pl
from jax.experimental.pallas import tpu as pltpu
from jax.sharding import PartitionSpec as P

F32, BF16 = jnp.float32, jnp.bfloat16
MESH = pl.DeviceIdType.MESH
N = 512
HALF = N // 2
VMEM_SPEC = pl.BlockSpec(memory_space=pltpu.VMEM)
ANY_SPEC = pl.BlockSpec(memory_space=pl.ANY)
SMEM_SPEC = pl.BlockSpec(memory_space=pltpu.SMEM)
LIMIT = 60 * 1024 * 1024
NN = ((1,), (0,))
NT = ((1,), (1,))


def dot(a, b, dims=NN, precision=None):
    return lax.dot_general(a, b, (dims, ((), ())), precision=precision, preferred_element_type=F32)


def split(x):
    high = x.astype(BF16)
    return high, (x - high.astype(F32)).astype(BF16)


def split3(x):
    high = x.astype(BF16)
    rest = x - high.astype(F32)
    middle = rest.astype(BF16)
    return high, middle, (rest - middle.astype(F32)).astype(BF16)


def mm3(a, b, dims=NN):
    return dot(a[0], b[0], dims) + (dot(a[0], b[1], dims) + dot(a[1], b[0], dims))


def mm6(a, b):
    small = dot(a[0], b[2]) + (dot(a[1], b[1]) + dot(a[2], b[0]))
    return dot(a[0], b[0]) + ((dot(a[0], b[1]) + dot(a[1], b[0])) + small)


def eye(rows=N, cols=N, offset=0):
    return (
        lax.broadcasted_iota(jnp.int32, (rows, cols), 0) + offset == lax.broadcasted_iota(jnp.int32, (rows, cols), 1)
    ).astype(F32)


def invert(m_ref, out_ref, xb, rb, mh, mm, ml, alpha, low, steps):
    m = m_ref[...]
    mh[...], mm[...], ml[...] = split3(m)
    grown = 4.0 / ((1.0 + low) * (1.0 + low))
    xb[...] = ((grown * alpha) * ((1.0 + low) * eye() - alpha * m)).astype(BF16)

    def step(index, low):
        factor = 4.0 / ((1.0 + low) * (1.0 + low))
        rb[...] = ((1.0 + low) * eye() - dot(mh[...], xb[...])).astype(BF16)
        later = factor * low
        scale = jnp.where(index == steps - 1, factor * (2.0 / (1.0 + later)), factor)
        xb[...] = (scale * dot(xb[...], rb[...])).astype(BF16)
        return later

    lax.fori_loop(0, steps, step, jnp.float32(grown * low))
    resid = (eye() - dot(mh[...], xb[...])) - (dot(mm[...], xb[...]) + dot(ml[...], xb[...]))
    size = jnp.sum(resid * resid)
    rb[...] = resid.astype(BF16)
    square = dot(rb[...], rb[...])
    square_size = jnp.sum(square * square)
    rb[...], mh[...] = split(resid + square)
    out_ref[...] = xb[...].astype(F32) + (dot(xb[...], rb[...]) + dot(xb[...], mh[...]))

    @pl.when(jnp.logical_not(square_size < 4e-7))
    def _():
        rows = 64
        highest = lax.Precision.HIGHEST

        def run(resid_ref):
            out_ref[...] = jnp.where(size < 0.8, xb[...].astype(F32), alpha * eye())

            def more(state):
                return jnp.logical_and(state[0] < 80, jnp.logical_not(state[1] < 1e-7))

            def again(state):
                def measure(i, total):
                    at = pl.ds(pl.multiple_of(i * rows, rows), rows)
                    part = eye(rows, N, i * rows) - dot(m_ref[at, :], out_ref[...], precision=highest)
                    resid_ref[at, :] = part
                    return total + jnp.sum(part * part)

                total = lax.fori_loop(0, N // rows, measure, jnp.float32(0.0))

                def update(i, carry):
                    at = pl.ds(pl.multiple_of(i * rows, rows), rows)
                    out_ref[at, :] = out_ref[at, :] + dot(out_ref[at, :], resid_ref[...], precision=highest)
                    return carry

                lax.fori_loop(0, N // rows, update, 0)
                return state[0] + 1, total

            lax.while_loop(more, again, (jnp.int32(0), jnp.float32(1e30)))

        pl.run_scoped(run, pltpu.VMEM((N, N), F32))


INVERT_SCRATCH = [pltpu.VMEM((N, N), BF16)] * 5


def call(kernel, out_shape, ins, scratch, **params):
    return pl.pallas_call(
        kernel,
        out_shape=out_shape,
        in_specs=ins,
        out_specs=jax.tree.map(lambda _: VMEM_SPEC, out_shape),
        scratch_shapes=scratch,
        compiler_params=pltpu.CompilerParams(vmem_limit_bytes=LIMIT, **params),
    )


def leaf_kernel(live_ref, rows_ref, values_ref, pattern_ref, q_ref, v_ref, w_ref, m_ref, *scratch):
    blocks, wide = pattern_ref.shape
    width = N // wide
    row_of = lax.broadcasted_iota(jnp.int32, (wide, N), 0)
    spread = (lax.broadcasted_iota(jnp.int32, (wide, N), 1) // width == row_of).astype(F32)
    keep = dot(pattern_ref[...].astype(F32), spread)
    keep = jnp.where(lax.broadcasted_iota(jnp.int32, (blocks, N), 0) < live_ref[0], keep, 0.0)
    size = N // blocks
    masked = jnp.concatenate(
        [rows_ref[i * size : (i + 1) * size, :] * keep[i : i + 1, :].astype(BF16) for i in range(blocks)], axis=0
    )
    m = dot(masked, masked, ((0,), (0,))) + q_ref[...]
    m_ref[...] = m
    vector = mm3_row(values_ref[...], masked)
    bound = jnp.max(jnp.sum(jnp.abs(m), axis=0, keepdims=True)) * 1.00001
    invert(m_ref, v_ref, *scratch, 1.0 / bound, 1.0 / 64.0, 4)
    w_ref[...] = mm3(split(vector), split(v_ref[...]))


def mm3_row(values, right):
    high, rest = split(values)
    low = (values - high.astype(F32) - rest.astype(F32)).astype(BF16)
    return dot(high, right) + (dot(rest, right) + dot(low, right))


def tier_body(first, s_ref, u_ref, q_ref, g_ref, w_ref, m_ref, scratch):
    if first:
        m_ref[...] = 5.0 * eye() - mm6(split3(s_ref[...]), split3(q_ref[...]))
    else:
        m_ref[...] = 5.0 * eye() - s_ref[...]
    invert(m_ref, g_ref, *scratch, 1.0 / 5.001, 0.1999, 2)
    w_ref[...] = mm3(split(u_ref[...]), split(g_ref[...]), NT)


def tier1_kernel(s_ref, u_ref, q_ref, v_ref, g_ref, w_ref, r_ref, m_ref, *scratch):
    tier_body(True, s_ref, u_ref, q_ref, g_ref, w_ref, m_ref, scratch)
    half = pl.ds(pl.multiple_of(lax.axis_index("blk") * HALF, HALF), HALF)
    r_ref[...] = mm3(split(g_ref[...]), split(v_ref[:, half]))


def tier_kernel(s_ref, u_ref, r_in_ref, g_ref, w_ref, r_ref, m_ref, *scratch):
    tier_body(False, s_ref, u_ref, None, g_ref, w_ref, m_ref, scratch)
    r_ref[...] = mm3(split(g_ref[...]), split(r_in_ref[...]))


def root_kernel(
    s_ref, u_ref, r4_ref, r3_ref, r2_ref, g3_ref, g2_ref, g1_ref, v_ref, q_ref, w3_ref, w2_ref, w1_ref, w0_ref,
    mean_ref, cov_ref, g_ref, w_ref, m_ref, *scratch,
):
    tier_body(False, s_ref, u_ref, None, g_ref, w_ref, m_ref, scratch)
    q = mm3(split(g_ref[...]), split(r4_ref[...]))
    mean = w_ref[...]
    for r_ref, w_n_ref, g_n_ref in ((r4_ref, w3_ref, g3_ref), (r3_ref, w2_ref, g2_ref), (r2_ref, w1_ref, g1_ref)):
        gain = split(g_n_ref[...])
        q = r_ref[...] + mm3(gain, split(q))
        mean = w_n_ref[...] + mm3(split(mean), gain, NT)
    v = split(v_ref[...])
    info = split(q_ref[...])
    half = pl.ds(pl.multiple_of(lax.axis_index("blk") * HALF, HALF), HALF)
    cov_ref[...] = v_ref[:, half] + mm3(v, split(mm3(info, split(q))))
    mean = w0_ref[...] + mm3(split(mm3(split(mean), info)), v)
    mean_ref[...] = mean[0:1, :]


def place(leaf):
    return leaf // 16, (leaf // 4) % 4, leaf % 4


def comm_kernel(tier, g_ref, w_ref, s_ref, u_ref, parts, vecs, full, sems, send_sems, local_sem):
    leaf, core = lax.axis_index("leaf"), lax.axis_index("blk")
    z, y, x = place(leaf)
    if tier == 0:
        mine, stride = x, 1
    elif tier == 1:
        mine, stride = y, 4
    elif tier == 2:
        mine, stride = z % 4, 16
    else:
        mine, stride = z // 4, 64
    base = leaf - mine * stride

    def sibling(k):
        return base + ((mine + k) % 4) * stride

    def along_y(k):
        return leaf - y * 4 + ((y + k) % 4) * 4

    def along_x(k):
        return leaf - x + (x + k) % 4

    gather_y = tier >= 2
    peers = [sibling(k) for k in (1, 2, 3)]
    if gather_y:
        peers += [along_y(k) for k in (1, 2, 3)]
    if tier >= 1:
        peers += [along_x(k) for k in (1, 2, 3)]
    barrier = pltpu.get_barrier_semaphore()
    for peer in peers:
        pl.semaphore_signal(barrier, inc=1, device_id=(peer, core), device_id_type=MESH)
    pl.semaphore_signal(barrier, inc=1, device_id=(leaf, 1 - core), device_id_type=MESH)
    pl.semaphore_wait(barrier, len(peers) + 1)

    count = 16 if gather_y else 64
    quarter = N // 8

    def rows(c, x_at, y_at=None):
        start = c * HALF + x_at * quarter
        if y_at is not None:
            return pl.ds(pl.multiple_of(start + y_at * 16, 16), 16)
        return pl.ds(pl.multiple_of(start, quarter), quarter)

    def remote(src, dst, index, device):
        return pltpu.make_async_remote_copy(
            src_ref=src, dst_ref=dst, send_sem=send_sems.at[index], recv_sem=sems.at[index],
            device_id=device, device_id_type=MESH,
        )

    if tier == 0:
        own = rows(core, x)
    elif gather_y:
        own = rows(core, x, y)
    else:
        own = rows(core, x)
    first = []
    for k in (1, 2, 3):
        source = rows(core, (x + k) % 4) if tier == 0 else own
        first.append(remote(g_ref.at[source, :], parts.at[mine], k - 1, (sibling(k), core)))
        first.append(remote(w_ref, vecs.at[mine], 2 + k, (sibling(k), core)))
    for copy in first:
        copy.start()
    keep = pltpu.make_async_copy(g_ref.at[own, :], parts.at[mine], local_sem.at[0])
    keep_vec = pltpu.make_async_copy(w_ref, vecs.at[mine], local_sem.at[1])
    keep.start()
    keep_vec.start()
    keep.wait()
    keep_vec.wait()
    for copy in first:
        copy.wait()
    full[own, :] = (parts[0] + parts[1]) + (parts[2] + parts[3])
    u_ref[...] = (vecs[0] + vecs[1]) + (vecs[2] + vecs[3])
    if gather_y:
        second = [remote(full.at[own, :], full.at[own, :], 5 + k, (along_y(k), core)) for k in (1, 2, 3)]
        for copy in second:
            copy.start()
        for copy in second:
            copy.wait()
    quarter_rows = rows(core, x)
    third = [remote(full.at[quarter_rows, :], full.at[quarter_rows, :], 8 + k, (along_x(k), core)) for k in (1, 2, 3)]
    for copy in third:
        copy.start()
    partner = (leaf, 1 - core)
    last = [remote(full.at[quarter_rows, :], full.at[quarter_rows, :], 12, partner)]
    last[0].start()
    for k in (1, 2, 3):
        third[k - 1].wait_recv()
        arrived = rows(core, (x + 4 - k) % 4)
        copy = remote(full.at[arrived, :], full.at[arrived, :], 12 + k, partner)
        copy.start()
        last.append(copy)
    for copy in third:
        copy.wait_send()
    for copy in last:
        copy.wait()
    s_ref[...] = full[...]


def comm(tier, g, w):
    count = 16 if tier >= 2 else 64
    return pl.pallas_call(
        functools.partial(comm_kernel, tier),
        out_shape=(jax.ShapeDtypeStruct((N, N), F32), jax.ShapeDtypeStruct((8, N), F32)),
        in_specs=[VMEM_SPEC, VMEM_SPEC],
        out_specs=(VMEM_SPEC, VMEM_SPEC),
        scratch_shapes=[
            pltpu.VMEM((4, count, N), F32),
            pltpu.VMEM((4, 8, N), F32),
            pltpu.VMEM((N, N), F32),
            pltpu.SemaphoreType.DMA((16,)),
            pltpu.SemaphoreType.DMA((16,)),
            pltpu.SemaphoreType.DMA((2,)),
        ],
        compiler_params=pltpu.CompilerParams(vmem_limit_bytes=LIMIT, collective_id=tier, has_side_effects=True),
    )(g, w)


def matrix(rows=N, cols=N, dtype=F32):
    return jax.ShapeDtypeStruct((rows, cols), dtype)


def leaf_call(obs_rows, obs_values, track_blocks, pattern, process_info):
    values = jnp.broadcast_to(obs_values[None, :], (8, N))
    return call(
        leaf_kernel, (matrix(), matrix(8)), [SMEM_SPEC] + [VMEM_SPEC] * 4, [pltpu.VMEM((N, N), F32)] + INVERT_SCRATCH
    )(track_blocks, obs_rows, values, pattern, process_info)


def tier1_call(s, u, q, v):
    return call(
        tier1_kernel, (matrix(), matrix(8), matrix(N, HALF)), [VMEM_SPEC] * 4, [pltpu.VMEM((N, N), F32)] + INVERT_SCRATCH
    )(s, u, q, v)


def tier_call(s, u, r):
    return call(
        tier_kernel, (matrix(), matrix(8), matrix(N, HALF)), [VMEM_SPEC] * 3, [pltpu.VMEM((N, N), F32)] + INVERT_SCRATCH
    )(s, u, r)


def root_call(*args):
    return call(
        root_kernel,
        (matrix(1), matrix(N, HALF)),
        [VMEM_SPEC] * 14,
        [pltpu.VMEM((N, N), F32), pltpu.VMEM((8, N), F32), pltpu.VMEM((N, N), F32)] + INVERT_SCRATCH,
    )(*args)


def shards(obs_rows, obs_values, track_blocks, pattern, process_info):
    v0, w0 = leaf_call(obs_rows, obs_values, track_blocks, pattern, process_info)
    s, u = comm(0, v0, w0)
    g1, w1, r2 = tier1_call(s, u, process_info, v0)
    s, u = comm(1, g1, w1)
    g2, w2, r3 = tier_call(s, u, r2)
    s, u = comm(2, g2, w2)
    g3, w3, r4 = tier_call(s, u, r3)
    s, u = comm(3, g3, w3)
    return root_call(s, u, r4, r3, r2, g3, g2, g1, v0, process_info, w3, w2, w1, w0)


def solution(mesh):
    placed = (P("leaf", None), P("leaf"), P("leaf"), P("leaf", None), P())
    return jax.shard_map(
        shards,
        mesh=mesh,
        in_specs=placed,
        out_specs=(P("leaf", None), P("leaf", "blk")),
        check_vma=False,
    )
```

```python
import functools

import jax
import jax.numpy as jnp
from jax import lax
from jax.experimental import pallas as pl
from jax.experimental.pallas import tpu as pltpu
from jax.sharding import PartitionSpec as P

F32, BF16 = jnp.float32, jnp.bfloat16
MESH = pl.DeviceIdType.MESH
N = 512
HALF = N // 2
VMEM_SPEC = pl.BlockSpec(memory_space=pltpu.VMEM)
ANY_SPEC = pl.BlockSpec(memory_space=pl.ANY)
SMEM_SPEC = pl.BlockSpec(memory_space=pltpu.SMEM)
LIMIT = 60 * 1024 * 1024
NN = ((1,), (0,))
NT = ((1,), (1,))


def dot(a, b, dims=NN, precision=None):
    return lax.dot_general(a, b, (dims, ((), ())), precision=precision, preferred_element_type=F32)


def split(x):
    high = x.astype(BF16)
    return high, (x - high.astype(F32)).astype(BF16)


def split3(x):
    high = x.astype(BF16)
    rest = x - high.astype(F32)
    middle = rest.astype(BF16)
    return high, middle, (rest - middle.astype(F32)).astype(BF16)


def mm3(a, b, dims=NN):
    return dot(a[0], b[0], dims) + (dot(a[0], b[1], dims) + dot(a[1], b[0], dims))


def mm6(a, b):
    small = dot(a[0], b[2]) + (dot(a[1], b[1]) + dot(a[2], b[0]))
    return dot(a[0], b[0]) + ((dot(a[0], b[1]) + dot(a[1], b[0])) + small)


def eye(rows=N, cols=N, offset=0):
    return (
        lax.broadcasted_iota(jnp.int32, (rows, cols), 0) + offset == lax.broadcasted_iota(jnp.int32, (rows, cols), 1)
    ).astype(F32)


def invert(m_ref, xb, rb, mh, mm, ml, alpha, low, steps):
    m = m_ref[...]
    mh[...], mm[...], ml[...] = split3(m)
    grown = 4.0 / ((1.0 + low) * (1.0 + low))
    xb[...] = ((grown * alpha) * ((1.0 + low) * eye() - alpha * m)).astype(BF16)

    def step(index, low):
        factor = 4.0 / ((1.0 + low) * (1.0 + low))
        rb[...] = ((1.0 + low) * eye() - dot(mh[...], xb[...])).astype(BF16)
        later = factor * low
        scale = jnp.where(index == steps - 1, factor * (2.0 / (1.0 + later)), factor)
        xb[...] = (scale * dot(xb[...], rb[...])).astype(BF16)
        return later

    lax.fori_loop(0, steps, step, jnp.float32(grown * low))
    resid = (eye() - dot(mh[...], xb[...])) - (dot(mm[...], xb[...]) + dot(ml[...], xb[...]))
    rb[...] = resid.astype(BF16)
    square = dot(rb[...], rb[...])
    rb[...], mh[...] = split(resid + square)
    return jnp.sum(square * square, keepdims=True)


def finish(out_ref, xb, rb, mh):
    out_ref[...] = xb[...].astype(F32) + (dot(xb[...], rb[...]) + dot(xb[...], mh[...]))


def mm3_row(values, right):
    high, rest, low = split3(values)
    return dot(high, right) + (dot(rest, right) + dot(low, right))


def flagged(vector, below, missed):
    row = lax.broadcasted_iota(jnp.int32, (8, N), 0)
    return jnp.where(row == 1, below + jnp.where(missed < 4e-7, 0.0, 1.0), jnp.where(row == 0, vector, 0.0))


def place(leaf):
    return leaf // 16, (leaf // 4) % 4, leaf % 4


def group(tier, leaf):
    z, y, x = place(leaf)
    return ((x, 1), (y, 4), (z % 4, 16), (z // 4, 64))[tier]


def ring(leaf, mine, stride, k):
    return leaf - mine * stride + ((mine + k) % 4) * stride


PARTNER = 21
SEMS = PARTNER + 8


def exchange(tier, g_ref, w_ref, parts, vecs, full, u_ref, send_sems, recv_sems, sent, meanwhile):
    leaf, core = lax.axis_index("leaf"), lax.axis_index("blk")
    z, y, x = place(leaf)
    mine, stride = group(tier, leaf)
    gather_y = tier >= 2
    eighth = N // 8

    def quarter(c, x_at):
        return pl.ds(pl.multiple_of(c * HALF + x_at * eighth, eighth), eighth)

    def cols(h):
        return pl.ds(h * HALF, HALF)

    def remote(src, dst, index, device):
        copy = pltpu.make_async_remote_copy(
            src_ref=src, dst_ref=dst, send_sem=send_sems.at[tier, index], recv_sem=recv_sems.at[tier, index],
            device_id=device, device_id_type=MESH,
        )
        copy.start()
        sent.append(copy)
        return copy

    def spread(rows, h, start, mine, stride):
        part = full.at[tier, rows, cols(h)]
        return [remote(part, part, start + 3 * h + k - 1, (ring(leaf, mine, stride, k), core)) for k in (1, 2, 3)]

    own = quarter(core, x)
    if gather_y:
        own = pl.ds(pl.multiple_of(core * HALF + x * eighth + y * 16, 16), 16)
    first = [[], []]
    for h in (0, 1):
        for k in (1, 2, 3):
            source = quarter(core, (x + k) % 4) if tier == 0 else own
            first[h].append(
                remote(
                    g_ref.at[source, cols(h)], parts.at[mine, :, cols(h)], 3 * h + k - 1,
                    (ring(leaf, mine, stride, k), core),
                )
            )
        if h == 0:
            vectors = [
                remote(w_ref, vecs.at[tier, mine], 5 + k, (ring(leaf, mine, stride, k), core)) for k in (1, 2, 3)
            ]
    parts[mine, :, :] = g_ref[own, :]
    vecs[tier, mine] = w_ref[...]
    meanwhile()
    along_y, along_x, halves = [], [], []

    def to_x(h):
        along_x.append(spread(quarter(core, x), h, 15, x, 1))
        to_partner(h, 0)

    def to_partner(h, k):
        part = full.at[tier, quarter(core, (x + 4 - k) % 4), cols(h)]
        halves.append(remote(part, part, PARTNER + 4 * h + k, (leaf, 1 - core)))

    for h in (0, 1):
        for copy in first[h]:
            copy.wait_recv()
        at = slice(h * HALF, (h + 1) * HALF)
        full[tier, own, at] = (parts[0, :, at] + parts[1, :, at]) + (parts[2, :, at] + parts[3, :, at])
        if gather_y:
            along_y.append(spread(own, h, 9, y, 4))
        else:
            to_x(h)
    for h in (0, 1):
        if gather_y:
            for copy in along_y[h]:
                copy.wait_recv()
            to_x(h)
    for copy in vectors:
        copy.wait_recv()
    u_ref[...] = (vecs[tier, 0] + vecs[tier, 1]) + (vecs[tier, 2] + vecs[tier, 3])
    for h in (0, 1):
        for k in (1, 3, 2):
            along_x[h][k - 1].wait_recv()
            to_partner(h, k)
    for copy in halves:
        copy.wait_recv()


def smoother_kernel(
    live_ref, rows_ref, values_ref, pattern_ref, q_ref, mean_ref, cov_ref, missed_ref,
    g, m_ref, xb, rb, mh, mm, ml, gh, gl, vh, vl, qh, ql, r, w, u_ref, full, vecs, parts0, parts1, parts2, parts3,
    send_sems, recv_sems,
):
    leaf, core = lax.axis_index("leaf"), lax.axis_index("blk")
    barrier = pltpu.get_barrier_semaphore()
    for tier in range(4):
        mine, stride = group(tier, leaf)
        for k in (1, 2, 3):
            peer = (ring(leaf, mine, stride, k), core)
            pl.semaphore_signal(barrier, inc=1, device_id=peer, device_id_type=MESH)
    pl.semaphore_signal(barrier, inc=1, device_id=(leaf, 1 - core), device_id_type=MESH)

    blocks, wide = pattern_ref.shape
    row_of = lax.broadcasted_iota(jnp.int32, (wide, N), 0)
    widen = (lax.broadcasted_iota(jnp.int32, (wide, N), 1) // (N // wide) == row_of).astype(F32)
    keep = dot(pattern_ref[...].astype(F32), widen)
    keep = jnp.where(lax.broadcasted_iota(jnp.int32, (blocks, N), 0) < live_ref[0], keep, 0.0)
    size = N // blocks
    masked = jnp.concatenate(
        [rows_ref[i * size : (i + 1) * size, :] * keep[i : i + 1, :].astype(BF16) for i in range(blocks)], axis=0
    )
    m = dot(masked, masked, ((0,), (0,))) + q_ref[...]
    m_ref[...] = m
    vector = mm3_row(jnp.broadcast_to(values_ref[...], (8, N)), masked)
    bound = jnp.max(jnp.sum(jnp.abs(m), axis=0, keepdims=True)) * 1.00001
    missed = invert(m_ref, xb, rb, mh, mm, ml, 1.0 / bound, 1.0 / 64.0, 4)
    v_ref = g.at[0]
    finish(v_ref, xb, rb, mh)
    vh[...], vl[...] = split(v_ref[...])
    w[0] = flagged(mm3(split(vector), (vh[...], vl[...])), 0.0, missed)
    pl.semaphore_wait(barrier, 13)

    half = pl.ds(pl.multiple_of(core * HALF, HALF), HALF)
    parts = (parts0, parts1, parts2, parts3)
    sent = []

    def meanwhile_leaf():
        qh[...], ql[...] = split(q_ref[...])
        r[0] = v_ref[:, half]

    def meanwhile_tier(n):
        def work():
            r[n] = mm3((gh[n - 1], gl[n - 1]), split(r[n - 1]))

        return work

    for tier in range(4):
        exchange(
            tier, g.at[tier], w.at[tier], parts[tier], vecs, full, u_ref, send_sems, recv_sems, sent,
            meanwhile_leaf if tier == 0 else meanwhile_tier(tier),
        )
        if tier == 0:
            m_ref[...] = 5.0 * eye() - mm6(split3(full[0]), split3(q_ref[...]))
        else:
            m_ref[...] = 5.0 * eye() - full[tier]
        missed = invert(m_ref, xb, rb, mh, mm, ml, 1.0 / 5.001, 0.1999, 2)
        u = u_ref[...]
        if tier < 3:
            g_ref = g.at[tier + 1]
            finish(g_ref, xb, rb, mh)
            gh[tier], gl[tier] = split(g_ref[...])
            w[tier + 1] = flagged(mm3(split(u), (gh[tier], gl[tier]), NT), u, missed)
        else:
            u = u + mm3(split(u), (rb[...], mh[...]), NT)
            uh, ul = split(u)
            mean = dot(uh, xb[...], NT) + dot(ul, xb[...], NT)
            missed_ref[...] = (u_ref[1:2, 0:128] + jnp.where(missed < 4e-7, 0.0, 1.0)) * jnp.ones((8, 128), F32)
            q = r[3] + mm3((rb[...], mh[...]), split(r[3]))
            q_high, q_low = split(q)
            q = dot(xb[...], q_high) + dot(xb[...], q_low)
    for n in (3, 2, 1):
        gain = (gh[n - 1], gl[n - 1])
        q = r[n] + mm3(gain, split(q))
        mean = w[n] + mm3(split(mean), gain, NT)
    info = (qh[...], ql[...])
    v = (vh[...], vl[...])
    cov_ref[...] = r[0] + mm3(v, split(mm3(info, split(q))))
    mean = w[0] + mm3(split(mm3(split(mean), info)), v)
    mean_ref[...] = mean[0:1, :]
    for copy in sent:
        copy.wait_send()


def matrix(rows=N, cols=N, dtype=F32):
    return jax.ShapeDtypeStruct((rows, cols), dtype)


def smoother(obs_rows, obs_values, track_blocks, pattern, process_info):
    def square(count, dtype):
        return pltpu.VMEM((count, N, N) if count > 1 else (N, N), dtype)

    return pl.pallas_call(
        smoother_kernel,
        out_shape=(matrix(1), matrix(N, HALF), matrix(8, 128)),
        in_specs=[SMEM_SPEC] + [VMEM_SPEC] * 4,
        out_specs=(VMEM_SPEC,) * 3,
        scratch_shapes=[
            square(4, F32), square(1, F32), *[square(1, BF16)] * 5, square(3, BF16), square(3, BF16), *[square(1, BF16)] * 4,
            pltpu.VMEM((4, N, HALF), F32), pltpu.VMEM((4, 8, N), F32), pltpu.VMEM((8, N), F32), square(4, F32),
            pltpu.VMEM((4, 4, 8, N), F32),
            *[pltpu.VMEM((4, rows, N), F32) for rows in (64, 64, 16, 16)],
            pltpu.SemaphoreType.DMA((4, SEMS)), pltpu.SemaphoreType.DMA((4, SEMS)),
        ],
        compiler_params=pltpu.CompilerParams(vmem_limit_bytes=LIMIT, collective_id=0, has_side_effects=True),
    )(track_blocks, obs_rows, obs_values[None, :], pattern, process_info)


ROWS = 64
DEPTH = 128


def chunk(i, size):
    return pl.ds(pl.multiple_of(i * size, size), size)


def careful_rows(left_ref, right_ref, at):
    def add(j, total):
        piece = dot(left_ref[at, chunk(j, DEPTH)], right_ref[chunk(j, DEPTH), :], precision=lax.Precision.HIGHEST)
        return total + piece

    return lax.fori_loop(0, N // DEPTH, add, jnp.zeros((ROWS, right_ref.shape[1]), F32))


def careful_inverse_kernel(alpha_ref, m_ref, out_ref, resid_ref):
    out_ref[...] = alpha_ref[0] * eye()

    def more(state):
        return jnp.logical_and(state[0] < 80, jnp.logical_not(state[1] < 1e-7))

    def again(state):
        def measure(i, total):
            at = chunk(i, ROWS)
            part = eye(ROWS, N, i * ROWS) - careful_rows(m_ref, out_ref, at)
            resid_ref[at, :] = part
            return total + jnp.sum(part * part)

        total = lax.fori_loop(0, N // ROWS, measure, jnp.float32(0.0))

        def update(i, carry):
            at = chunk(i, ROWS)
            out_ref[at, :] = out_ref[at, :] + careful_rows(out_ref, resid_ref, at)
            return carry

        lax.fori_loop(0, N // ROWS, update, 0)
        return state[0] + 1, total

    lax.while_loop(more, again, (jnp.int32(0), jnp.float32(1e30)))


def careful_inverse(m, alpha):
    return pl.pallas_call(
        careful_inverse_kernel,
        out_shape=matrix(),
        in_specs=[SMEM_SPEC, VMEM_SPEC],
        out_specs=VMEM_SPEC,
        scratch_shapes=[pltpu.VMEM((N, N), F32)],
        compiler_params=pltpu.CompilerParams(vmem_limit_bytes=LIMIT),
    )(jnp.reshape(alpha, (1,)), m)


def careful_product_kernel(left_ref, right_ref, out_ref):
    def work(i, carry):
        at = chunk(i, ROWS)
        out_ref[at, :] = careful_rows(left_ref, right_ref, at)
        return carry

    lax.fori_loop(0, N // ROWS, work, 0)


def careful_product(left, right):
    return pl.pallas_call(
        careful_product_kernel,
        out_shape=matrix(N, right.shape[1]),
        in_specs=[VMEM_SPEC, VMEM_SPEC],
        out_specs=VMEM_SPEC,
        compiler_params=pltpu.CompilerParams(vmem_limit_bytes=LIMIT),
    )(left, right)


def comm_kernel(tier, g_ref, w_ref, s_ref, u_ref, parts, vecs, full, sems, send_sems, local_sem):
    leaf, core = lax.axis_index("leaf"), lax.axis_index("blk")
    z, y, x = place(leaf)
    if tier == 0:
        mine, stride = x, 1
    elif tier == 1:
        mine, stride = y, 4
    elif tier == 2:
        mine, stride = z % 4, 16
    else:
        mine, stride = z // 4, 64
    base = leaf - mine * stride

    def sibling(k):
        return base + ((mine + k) % 4) * stride

    def along_y(k):
        return leaf - y * 4 + ((y + k) % 4) * 4

    def along_x(k):
        return leaf - x + (x + k) % 4

    gather_y = tier >= 2
    peers = [sibling(k) for k in (1, 2, 3)]
    if gather_y:
        peers += [along_y(k) for k in (1, 2, 3)]
    if tier >= 1:
        peers += [along_x(k) for k in (1, 2, 3)]
    barrier = pltpu.get_barrier_semaphore()
    for peer in peers:
        pl.semaphore_signal(barrier, inc=1, device_id=(peer, core), device_id_type=MESH)
    pl.semaphore_signal(barrier, inc=1, device_id=(leaf, 1 - core), device_id_type=MESH)
    pl.semaphore_wait(barrier, len(peers) + 1)

    count = 16 if gather_y else 64
    quarter = N // 8

    def rows(c, x_at, y_at=None):
        start = c * HALF + x_at * quarter
        if y_at is not None:
            return pl.ds(pl.multiple_of(start + y_at * 16, 16), 16)
        return pl.ds(pl.multiple_of(start, quarter), quarter)

    def remote(src, dst, index, device):
        return pltpu.make_async_remote_copy(
            src_ref=src, dst_ref=dst, send_sem=send_sems.at[index], recv_sem=sems.at[index],
            device_id=device, device_id_type=MESH,
        )

    if tier == 0:
        own = rows(core, x)
    elif gather_y:
        own = rows(core, x, y)
    else:
        own = rows(core, x)
    first = []
    for k in (1, 2, 3):
        source = rows(core, (x + k) % 4) if tier == 0 else own
        first.append(remote(g_ref.at[source, :], parts.at[mine], k - 1, (sibling(k), core)))
        first.append(remote(w_ref, vecs.at[mine], 2 + k, (sibling(k), core)))
    for copy in first:
        copy.start()
    keep = pltpu.make_async_copy(g_ref.at[own, :], parts.at[mine], local_sem.at[0])
    keep_vec = pltpu.make_async_copy(w_ref, vecs.at[mine], local_sem.at[1])
    keep.start()
    keep_vec.start()
    keep.wait()
    keep_vec.wait()
    for copy in first:
        copy.wait()
    full[own, :] = (parts[0] + parts[1]) + (parts[2] + parts[3])
    u_ref[...] = (vecs[0] + vecs[1]) + (vecs[2] + vecs[3])
    if gather_y:
        second = [remote(full.at[own, :], full.at[own, :], 5 + k, (along_y(k), core)) for k in (1, 2, 3)]
        for copy in second:
            copy.start()
        for copy in second:
            copy.wait()
    quarter_rows = rows(core, x)
    third = [remote(full.at[quarter_rows, :], full.at[quarter_rows, :], 8 + k, (along_x(k), core)) for k in (1, 2, 3)]
    for copy in third:
        copy.start()
    partner = (leaf, 1 - core)
    last = [remote(full.at[quarter_rows, :], full.at[quarter_rows, :], 12, partner)]
    last[0].start()
    for k in (1, 2, 3):
        third[k - 1].wait_recv()
        arrived = rows(core, (x + 4 - k) % 4)
        copy = remote(full.at[arrived, :], full.at[arrived, :], 12 + k, partner)
        copy.start()
        last.append(copy)
    for copy in third:
        copy.wait_send()
    for copy in last:
        copy.wait()
    s_ref[...] = full[...]


def comm(tier, g, w):
    count = 16 if tier >= 2 else 64
    return pl.pallas_call(
        functools.partial(comm_kernel, tier),
        out_shape=(jax.ShapeDtypeStruct((N, N), F32), jax.ShapeDtypeStruct((8, N), F32)),
        in_specs=[VMEM_SPEC, VMEM_SPEC],
        out_specs=(VMEM_SPEC, VMEM_SPEC),
        scratch_shapes=[
            pltpu.VMEM((4, count, N), F32),
            pltpu.VMEM((4, 8, N), F32),
            pltpu.VMEM((N, N), F32),
            pltpu.SemaphoreType.DMA((16,)),
            pltpu.SemaphoreType.DMA((16,)),
            pltpu.SemaphoreType.DMA((2,)),
        ],
        compiler_params=pltpu.CompilerParams(vmem_limit_bytes=LIMIT, collective_id=tier + 1, has_side_effects=True),
    )(g, w)


def careful(obs_rows, obs_values, track_blocks, pattern, process_info):
    blocks, wide = pattern.shape
    keep = jnp.repeat(pattern.astype(BF16), N // wide, axis=1)
    keep = keep * (jnp.arange(blocks) < track_blocks[0]).astype(BF16)[:, None]
    masked = (obs_rows.reshape(blocks, -1, N) * keep[:, None, :]).reshape(-1, N)
    m = jnp.dot(masked.T, masked, preferred_element_type=F32) + process_info
    v = careful_inverse(m, 1.0 / (jnp.max(jnp.sum(jnp.abs(m), axis=0)) * 1.00001))

    def column(vector):
        return jnp.broadcast_to(vector[:, None], (N, 128))

    w0 = careful_product(v, careful_product(masked.T.astype(F32), column(obs_values)))
    g, w = v, w0
    r0 = lax.dynamic_slice_in_dim(v, lax.axis_index("blk") * HALF, HALF, 1)
    r, gains, kept = r0, [], []
    for tier in range(4):
        s, u = comm(tier, g, jnp.broadcast_to(w[:, 0][None, :], (8, N)))
        if tier == 0:
            s = careful_product(s, process_info)
        g = careful_inverse(5.0 * jnp.eye(N, dtype=F32) - s, jnp.float32(1.0 / 5.001))
        both = careful_product(g, jnp.concatenate([r, column(u[0])], axis=1))
        r, w = both[:, :HALF], both[:, HALF:]
        gains.append(g)
        kept.append(both)

    def down(state, of_tier):
        gain, own = of_tier
        return own + careful_product(gain, state), None

    state, _ = lax.scan(down, kept[3], (jnp.stack(gains[2::-1]), jnp.stack(kept[2::-1])))
    state = careful_product(v, careful_product(process_info, state))
    return (w0[:, 0] + state[:, HALF])[None, :], r0 + state[:, :HALF]


def shards(*args):
    mean, cov, missed = smoother(*args)
    return lax.cond(missed[0, 0] > 0.5, lambda: careful(*args), lambda: (mean, cov))


def solution(mesh):
    placed = (P("leaf", None), P("leaf"), P("leaf"), P("leaf", None), P())
    return jax.shard_map(
        shards,
        mesh=mesh,
        in_specs=placed,
        out_specs=(P("leaf", None), P("leaf", "blk")),
        check_vma=False,
    )
```

```python
import functools

import jax
import jax.numpy as jnp
from jax import lax
from jax.experimental import pallas as pl
from jax.experimental.pallas import tpu as pltpu
from jax.sharding import PartitionSpec as P

F32, BF16 = jnp.float32, jnp.bfloat16
MESH = pl.DeviceIdType.MESH
N = 512
HALF = N // 2
VMEM_SPEC = pl.BlockSpec(memory_space=pltpu.VMEM)
ANY_SPEC = pl.BlockSpec(memory_space=pl.ANY)
SMEM_SPEC = pl.BlockSpec(memory_space=pltpu.SMEM)
LIMIT = 60 * 1024 * 1024
NN = ((1,), (0,))
NT = ((1,), (1,))


def dot(a, b, dims=NN, precision=None):
    return lax.dot_general(a, b, (dims, ((), ())), precision=precision, preferred_element_type=F32)


def split(x):
    high = x.astype(BF16)
    return high, (x - high.astype(F32)).astype(BF16)


def split3(x):
    high = x.astype(BF16)
    rest = x - high.astype(F32)
    middle = rest.astype(BF16)
    return high, middle, (rest - middle.astype(F32)).astype(BF16)


def mm3(a, b, dims=NN):
    return dot(a[0], b[0], dims) + (dot(a[0], b[1], dims) + dot(a[1], b[0], dims))


def mm6(a, b):
    small = dot(a[0], b[2]) + (dot(a[1], b[1]) + dot(a[2], b[0]))
    return dot(a[0], b[0]) + ((dot(a[0], b[1]) + dot(a[1], b[0])) + small)


def eye(rows=N, cols=N, offset=0):
    return (
        lax.broadcasted_iota(jnp.int32, (rows, cols), 0) + offset == lax.broadcasted_iota(jnp.int32, (rows, cols), 1)
    ).astype(F32)


def invert(m_ref, xb, rb, mh, mm, ml, alpha, low, steps):
    m = m_ref[...]
    mh[...], mm[...], ml[...] = split3(m)
    grown = 4.0 / ((1.0 + low) * (1.0 + low))
    xb[...] = ((grown * alpha) * ((1.0 + low) * eye() - alpha * m)).astype(BF16)

    def step(index, low):
        factor = 4.0 / ((1.0 + low) * (1.0 + low))
        rb[...] = ((1.0 + low) * eye() - dot(mh[...], xb[...])).astype(BF16)
        later = factor * low
        scale = jnp.where(index == steps - 1, factor * (2.0 / (1.0 + later)), factor)
        xb[...] = (scale * dot(xb[...], rb[...])).astype(BF16)
        return later

    lax.fori_loop(0, steps, step, jnp.float32(grown * low))


def residual(m_ref, xb, rb, mh, mm):
    m_ref[...] = (eye() - dot(xb[...], mh[...])) - dot(xb[...], mm[...])
    rb[...] = m_ref[...].astype(BF16)


def inverse_rows(m_ref, xb, rb, ml, start, count):
    at = pl.ds(pl.multiple_of(start, 16), count)
    x_rows = xb[at, :]
    t = (m_ref[at, :] - dot(x_rows, ml[...])) + dot(rb[at, :], rb[...])
    both = dot(jnp.concatenate(split(t), axis=0), xb[...])
    return x_rows.astype(F32) + (both[:count] + both[count:])


def inverse_whole(m_ref, xb, rb, mh, ml):
    square = dot(rb[...], rb[...])
    rb[...], mh[...] = split((m_ref[...] - dot(xb[...], ml[...])) + square)
    whole = xb[...].astype(F32) + (dot(rb[...], xb[...]) + dot(mh[...], xb[...]))
    return whole, jnp.sum(square * square, keepdims=True)


def mm3_row(values, right):
    high, rest, low = split3(values)
    return dot(high, right) + (dot(rest, right) + dot(low, right))


def flagged(vector, below, missed):
    row = lax.broadcasted_iota(jnp.int32, (8, N), 0)
    return jnp.where(row == 1, below + jnp.where(missed < 4e-7, 0.0, 1.0), jnp.where(row == 0, vector, 0.0))


def place(leaf):
    return leaf // 16, (leaf // 4) % 4, leaf % 4


def group(tier, leaf):
    z, y, x = place(leaf)
    return ((x, 1), (y, 4), (z % 4, 16), (z // 4, 64))[tier]


def ring(leaf, mine, stride, k):
    return leaf - mine * stride + ((mine + k) % 4) * stride


def observe(live_ref, rows_ref, values_ref, pattern_ref, q_ref):
    blocks, wide = pattern_ref.shape
    row_of = lax.broadcasted_iota(jnp.int32, (wide, N), 0)
    widen = (lax.broadcasted_iota(jnp.int32, (wide, N), 1) // (N // wide) == row_of).astype(F32)
    keep = dot(pattern_ref[...].astype(F32), widen)
    keep = jnp.where(lax.broadcasted_iota(jnp.int32, (blocks, N), 0) < live_ref[0], keep, 0.0)
    size = N // blocks
    masked = jnp.concatenate(
        [rows_ref[i * size : (i + 1) * size, :] * keep[i : i + 1, :].astype(BF16) for i in range(blocks)], axis=0
    )
    vector = mm3_row(jnp.broadcast_to(values_ref[...], (8, N)), masked)
    return dot(masked, masked, ((0,), (0,))) + q_ref[...], vector


VECTOR, PHASE_A, PHASE_B, PARTNER = 6, 9, 15, 21
SEMS = PARTNER + 8


def exchange(tier, send, w_ref, parts, vecs, full, u_ref, send_sems, recv_sems, sent, first_work, second_work):
    leaf, core = lax.axis_index("leaf"), lax.axis_index("blk")
    z, y, x = place(leaf)
    mine, stride = group(tier, leaf)
    strip = core * 4 + x
    strips = pl.ds(core * 4, 4)

    def cols(h):
        return pl.ds(h * HALF, HALF)

    def remote(src, dst, index, device):
        copy = pltpu.make_async_remote_copy(
            src_ref=src, dst_ref=dst, send_sem=send_sems.at[tier, index], recv_sem=recv_sems.at[tier, index],
            device_id=device, device_id_type=MESH,
        )
        copy.start()
        sent.append(copy)
        return copy

    def spread(part, start, mine, stride):
        return [remote(part, part, start + k - 1, (ring(leaf, mine, stride, k), core)) for k in (1, 2, 3)]

    def to_partner(h, j, part):
        halves.append(remote(part, part, PARTNER + 4 * h + j, (leaf, 1 - core)))

    first, halves = [[], []], []
    for h in (0, 1):
        for k in (1, 2, 3):
            device = (ring(leaf, mine, stride, k), core)
            if tier == 0:
                src, dst = send.at[(mine + k) % 4, :, :, cols(h)], parts.at[mine, :, :, cols(h)]
            elif tier == 1:
                src, dst = send.at[(mine + k) % 4, :, cols(h)], parts.at[mine, :, cols(h)]
            else:
                src, dst = send.at[:, cols(h)], parts.at[mine, :, cols(h)]
            first[h].append(remote(src, dst, 3 * h + k - 1, device))
    parts[mine] = send[mine] if tier < 2 else send[...]
    first_work()
    vecs[tier, mine] = w_ref[...]
    vectors = [
        remote(w_ref, vecs.at[tier, mine], VECTOR + k - 1, (ring(leaf, mine, stride, k), core)) for k in (1, 2, 3)
    ]
    along = {}

    def strip_part(h, number):
        return full.at[tier, number, :, :, cols(h)]

    def level_part(h, number):
        return full.at[tier, strips, number, :, cols(h)]

    for h in (0, 1):
        for copy in first[h]:
            copy.wait_recv()
        at = slice(h * HALF, (h + 1) * HALF)
        total = (parts[0, ..., at] + parts[1, ..., at]) + (parts[2, ..., at] + parts[3, ..., at])
        if tier == 0:
            full[tier, strip, :, :, at] = total
            along[h] = spread(strip_part(h, strip), PHASE_B + 3 * h, x, 1)
            to_partner(h, 0, strip_part(h, strip))
        else:
            full[tier, strip, y, :, at] = total
            own = full.at[tier, strip, y, :, cols(h)]
            along[h] = spread(own, PHASE_A, y, 4) if h == 0 else spread(own, PHASE_A + 3, x, 1)
    second_work()
    if tier > 0:
        for copy in along[0]:
            copy.wait_recv()
        along[0] = spread(strip_part(0, strip), PHASE_B, x, 1)
        for copy in along[1]:
            copy.wait_recv()
        along[1] = spread(level_part(1, y), PHASE_B + 3, y, 4)
        to_partner(0, 0, strip_part(0, strip))
        to_partner(1, 0, level_part(1, y))
    for k in (1, 3, 2):
        for h in (0, 1):
            along[h][k - 1].wait_recv()
            if tier == 0 or h == 0:
                to_partner(h, k, strip_part(h, core * 4 + (x + 4 - k) % 4))
            else:
                to_partner(h, k, level_part(h, (y + 4 - k) % 4))
    for copy in halves:
        copy.wait_recv()
    for copy in vectors:
        copy.wait_recv()
    u_ref[...] = (vecs[tier, 0] + vecs[tier, 1]) + (vecs[tier, 2] + vecs[tier, 3])


def smoother_kernel(
    live_ref, rows_ref, values_ref, pattern_ref, q_ref, mean_ref, near_ref, far_ref, missed_ref,
    m_ref, xb, rb, mh, mm, ml, gh, gl, hh, hl, vector_ref, r, mean_acc, w, u_ref, full, vecs,
    send0, send1, send2, send3, parts0, parts1, parts2, parts3, send_sems, recv_sems,
):
    leaf, core = lax.axis_index("leaf"), lax.axis_index("blk")
    z, y, x = place(leaf)
    barrier = pltpu.get_barrier_semaphore()
    for tier in range(4):
        mine, stride = group(tier, leaf)
        for k in (1, 2, 3):
            peer = (ring(leaf, mine, stride, k), core)
            pl.semaphore_signal(barrier, inc=1, device_id=peer, device_id_type=MESH)
    pl.semaphore_signal(barrier, inc=1, device_id=(leaf, 1 - core), device_id_type=MESH)

    m, vector_ref[...] = observe(live_ref, rows_ref, values_ref, pattern_ref, q_ref)
    m_ref[...] = m
    bound = jnp.max(jnp.sum(jnp.abs(m), axis=0, keepdims=True)) * 1.00001
    invert(m_ref, xb, rb, mh, mm, ml, 1.0 / bound, 1.0 / 64.0, 4)
    residual(m_ref, xb, rb, mh, mm)
    send0[...] = inverse_rows(m_ref, xb, rb, ml, core * HALF, HALF).reshape(4, 4, 16, N)
    pl.semaphore_wait(barrier, 13)

    def leaf_first():
        v, missed = inverse_whole(m_ref, xb, rb, mh, ml)
        gh[...], gl[...] = split(v)
        w[0] = flagged(mm3(split(vector_ref[...]), (gh[...], gl[...])), 0.0, missed)
        mean_acc[...] = w[0]
        near_ref[...] = send0[...].reshape(HALF, N).T
        r[...] = near_ref[...]

    def leaf_second():
        hh[...], hl[...] = split(mm3((gh[...], gl[...]), split(q_ref[...])))

    def tier_first(n):
        def work():
            gain, missed = inverse_whole(m_ref, xb, rb, mh, ml)
            gh[...], gl[...] = split(gain)
            u = u_ref[...]
            w[n] = flagged(mm3(split(u), (gh[...], gl[...]), NT), u, missed)

        return work

    def tier_second(n):
        def work():
            r[...] = mm3((gh[...], gl[...]), split(r[...]))
            near_ref[...] += mm3((hh[...], hl[...]), split(r[...]))
            mean_acc[...] += mm3(split(w[n]), (hh[...], hl[...]), NT)
            hh[...], hl[...] = split(mm3((hh[...], hl[...]), (gh[...], gl[...])))

        return work

    sends = (send0, send1, send2, send3)
    parts = (parts0, parts1, parts2, parts3)
    sent = []
    for tier in range(4):
        exchange(
            tier, sends[tier], w.at[tier], parts[tier], vecs, full, u_ref, send_sems, recv_sems, sent,
            leaf_first if tier == 0 else tier_first(tier), leaf_second if tier == 0 else tier_second(tier),
        )
        total = full[tier].reshape(N, N)
        if tier == 0:
            m_ref[...] = 5.0 * eye() - mm6(split3(total), split3(q_ref[...]))
        else:
            m_ref[...] = 5.0 * eye() - total
        invert(m_ref, xb, rb, mh, mm, ml, 1.0 / 5.001, 0.1999, 2)
        if tier < 3:
            residual(m_ref, xb, rb, mh, mm)
        if tier == 0:
            start = core * HALF + x * 64
            send1[...] = inverse_rows(m_ref, xb, rb, ml, start, 64).reshape(4, 16, N)
        elif tier < 3:
            start = core * HALF + x * 64 + y * 16
            sends[tier + 1][...] = inverse_rows(m_ref, xb, rb, ml, start, 16)
    resid = (eye() - dot(mh[...], xb[...])) - (dot(mm[...], xb[...]) + dot(ml[...], xb[...]))
    rb[...] = resid.astype(BF16)
    square = dot(rb[...], rb[...])
    rb[...], mh[...] = split(resid + square)
    missed = jnp.where(jnp.sum(square * square, keepdims=True) < 4e-7, 0.0, 1.0)
    missed_ref[0] = jnp.max(u_ref[1:2, 0:128] + missed)
    q = r[...] + mm3((rb[...], mh[...]), split(r[...]))
    q_high, q_low = split(q)
    q = dot(xb[...], q_high) + dot(xb[...], q_low)
    far_ref[...] = mm3((hh[...], hl[...]), split(q))
    u = u_ref[...]
    u = u + mm3(split(u), (rb[...], mh[...]), NT)
    u_high, u_low = split(u)
    mean = dot(u_high, xb[...], NT) + dot(u_low, xb[...], NT)
    mean = mean_acc[...] + mm3(split(mean), (hh[...], hl[...]), NT)
    mean_ref[...] = mean[0:1, :]
    for copy in sent:
        copy.wait_send()


def matrix(rows=N, cols=N, dtype=F32):
    return jax.ShapeDtypeStruct((rows, cols), dtype)


def smoother(obs_rows, obs_values, track_blocks, pattern, process_info):
    def square(dtype):
        return pltpu.VMEM((N, N), dtype)

    vector = pltpu.VMEM((8, N), F32)
    pieces = [(4, 16, N), (16, N), (16, N), (16, N)]
    sends = [(4, 4, 16, N), (4, 16, N), (16, N), (16, N)]
    return pl.pallas_call(
        smoother_kernel,
        out_shape=(matrix(1), matrix(N, HALF), matrix(N, HALF), jax.ShapeDtypeStruct((1,), F32)),
        in_specs=[SMEM_SPEC] + [VMEM_SPEC] * 4,
        out_specs=(VMEM_SPEC,) * 3 + (SMEM_SPEC,),
        scratch_shapes=[
            square(F32), *[square(BF16)] * 9, vector, pltpu.VMEM((N, HALF), F32), vector, pltpu.VMEM((4, 8, N), F32), vector,
            pltpu.VMEM((4, 8, 4, 16, N), F32), pltpu.VMEM((4, 4, 8, N), F32),
            *[pltpu.VMEM(shape, F32) for shape in sends], *[pltpu.VMEM((4, *shape), F32) for shape in pieces],
            pltpu.SemaphoreType.DMA((4, SEMS)), pltpu.SemaphoreType.DMA((4, SEMS)),
        ],
        compiler_params=pltpu.CompilerParams(vmem_limit_bytes=LIMIT, collective_id=0, has_side_effects=True),
    )(track_blocks, obs_rows, obs_values[None, :], pattern, process_info)


ROWS = 64
DEPTH = 128


def chunk(i, size):
    return pl.ds(pl.multiple_of(i * size, size), size)


def careful_rows(left_ref, right_ref, at):
    def add(j, total):
        piece = dot(left_ref[at, chunk(j, DEPTH)], right_ref[chunk(j, DEPTH), :], precision=lax.Precision.HIGHEST)
        return total + piece

    return lax.fori_loop(0, N // DEPTH, add, jnp.zeros((ROWS, right_ref.shape[1]), F32))


def careful_inverse_kernel(alpha_ref, m_ref, out_ref, resid_ref):
    out_ref[...] = alpha_ref[0] * eye()

    def more(state):
        return jnp.logical_and(state[0] < 80, jnp.logical_not(state[1] < 1e-7))

    def again(state):
        def measure(i, total):
            at = chunk(i, ROWS)
            part = eye(ROWS, N, i * ROWS) - careful_rows(m_ref, out_ref, at)
            resid_ref[at, :] = part
            return total + jnp.sum(part * part)

        total = lax.fori_loop(0, N // ROWS, measure, jnp.float32(0.0))

        def update(i, carry):
            at = chunk(i, ROWS)
            out_ref[at, :] = out_ref[at, :] + careful_rows(out_ref, resid_ref, at)
            return carry

        lax.fori_loop(0, N // ROWS, update, 0)
        return state[0] + 1, total

    lax.while_loop(more, again, (jnp.int32(0), jnp.float32(1e30)))


def careful_inverse(m, alpha):
    return pl.pallas_call(
        careful_inverse_kernel,
        out_shape=matrix(),
        in_specs=[SMEM_SPEC, VMEM_SPEC],
        out_specs=VMEM_SPEC,
        scratch_shapes=[pltpu.VMEM((N, N), F32)],
        compiler_params=pltpu.CompilerParams(vmem_limit_bytes=LIMIT),
    )(jnp.reshape(alpha, (1,)), m)


def careful_product_kernel(left_ref, right_ref, out_ref):
    def work(i, carry):
        at = chunk(i, ROWS)
        out_ref[at, :] = careful_rows(left_ref, right_ref, at)
        return carry

    lax.fori_loop(0, N // ROWS, work, 0)


def careful_product(left, right):
    return pl.pallas_call(
        careful_product_kernel,
        out_shape=matrix(N, right.shape[1]),
        in_specs=[VMEM_SPEC, VMEM_SPEC],
        out_specs=VMEM_SPEC,
        compiler_params=pltpu.CompilerParams(vmem_limit_bytes=LIMIT),
    )(left, right)


def comm_kernel(tier, g_ref, w_ref, s_ref, u_ref, parts, vecs, full, sems, send_sems, local_sem):
    leaf, core = lax.axis_index("leaf"), lax.axis_index("blk")
    z, y, x = place(leaf)
    if tier == 0:
        mine, stride = x, 1
    elif tier == 1:
        mine, stride = y, 4
    elif tier == 2:
        mine, stride = z % 4, 16
    else:
        mine, stride = z // 4, 64
    base = leaf - mine * stride

    def sibling(k):
        return base + ((mine + k) % 4) * stride

    def along_y(k):
        return leaf - y * 4 + ((y + k) % 4) * 4

    def along_x(k):
        return leaf - x + (x + k) % 4

    gather_y = tier >= 2
    peers = [sibling(k) for k in (1, 2, 3)]
    if gather_y:
        peers += [along_y(k) for k in (1, 2, 3)]
    if tier >= 1:
        peers += [along_x(k) for k in (1, 2, 3)]
    barrier = pltpu.get_barrier_semaphore()
    for peer in peers:
        pl.semaphore_signal(barrier, inc=1, device_id=(peer, core), device_id_type=MESH)
    pl.semaphore_signal(barrier, inc=1, device_id=(leaf, 1 - core), device_id_type=MESH)
    pl.semaphore_wait(barrier, len(peers) + 1)

    count = 16 if gather_y else 64
    quarter = N // 8

    def rows(c, x_at, y_at=None):
        start = c * HALF + x_at * quarter
        if y_at is not None:
            return pl.ds(pl.multiple_of(start + y_at * 16, 16), 16)
        return pl.ds(pl.multiple_of(start, quarter), quarter)

    def remote(src, dst, index, device):
        return pltpu.make_async_remote_copy(
            src_ref=src, dst_ref=dst, send_sem=send_sems.at[index], recv_sem=sems.at[index],
            device_id=device, device_id_type=MESH,
        )

    if tier == 0:
        own = rows(core, x)
    elif gather_y:
        own = rows(core, x, y)
    else:
        own = rows(core, x)
    first = []
    for k in (1, 2, 3):
        source = rows(core, (x + k) % 4) if tier == 0 else own
        first.append(remote(g_ref.at[source, :], parts.at[mine], k - 1, (sibling(k), core)))
        first.append(remote(w_ref, vecs.at[mine], 2 + k, (sibling(k), core)))
    for copy in first:
        copy.start()
    keep = pltpu.make_async_copy(g_ref.at[own, :], parts.at[mine], local_sem.at[0])
    keep_vec = pltpu.make_async_copy(w_ref, vecs.at[mine], local_sem.at[1])
    keep.start()
    keep_vec.start()
    keep.wait()
    keep_vec.wait()
    for copy in first:
        copy.wait()
    full[own, :] = (parts[0] + parts[1]) + (parts[2] + parts[3])
    u_ref[...] = (vecs[0] + vecs[1]) + (vecs[2] + vecs[3])
    if gather_y:
        second = [remote(full.at[own, :], full.at[own, :], 5 + k, (along_y(k), core)) for k in (1, 2, 3)]
        for copy in second:
            copy.start()
        for copy in second:
            copy.wait()
    quarter_rows = rows(core, x)
    third = [remote(full.at[quarter_rows, :], full.at[quarter_rows, :], 8 + k, (along_x(k), core)) for k in (1, 2, 3)]
    for copy in third:
        copy.start()
    partner = (leaf, 1 - core)
    last = [remote(full.at[quarter_rows, :], full.at[quarter_rows, :], 12, partner)]
    last[0].start()
    for k in (1, 2, 3):
        third[k - 1].wait_recv()
        arrived = rows(core, (x + 4 - k) % 4)
        copy = remote(full.at[arrived, :], full.at[arrived, :], 12 + k, partner)
        copy.start()
        last.append(copy)
    for copy in third:
        copy.wait_send()
    for copy in last:
        copy.wait()
    s_ref[...] = full[...]


def comm(tier, g, w):
    count = 16 if tier >= 2 else 64
    return pl.pallas_call(
        functools.partial(comm_kernel, tier),
        out_shape=(jax.ShapeDtypeStruct((N, N), F32), jax.ShapeDtypeStruct((8, N), F32)),
        in_specs=[VMEM_SPEC, VMEM_SPEC],
        out_specs=(VMEM_SPEC, VMEM_SPEC),
        scratch_shapes=[
            pltpu.VMEM((4, count, N), F32),
            pltpu.VMEM((4, 8, N), F32),
            pltpu.VMEM((N, N), F32),
            pltpu.SemaphoreType.DMA((16,)),
            pltpu.SemaphoreType.DMA((16,)),
            pltpu.SemaphoreType.DMA((2,)),
        ],
        compiler_params=pltpu.CompilerParams(vmem_limit_bytes=LIMIT, collective_id=tier + 1, has_side_effects=True),
    )(g, w)


def careful_leaf_kernel(live_ref, rows_ref, values_ref, pattern_ref, q_ref, m_ref, vector_ref):
    m_ref[...], vector_ref[...] = observe(live_ref, rows_ref, values_ref, pattern_ref, q_ref)


def careful(obs_rows, obs_values, track_blocks, pattern, process_info):
    m, vector = pl.pallas_call(
        careful_leaf_kernel,
        out_shape=(matrix(), matrix(8)),
        in_specs=[SMEM_SPEC] + [VMEM_SPEC] * 4,
        out_specs=(VMEM_SPEC,) * 2,
        compiler_params=pltpu.CompilerParams(vmem_limit_bytes=LIMIT),
    )(track_blocks, obs_rows, obs_values[None, :], pattern, process_info)
    v = careful_inverse(m, 1.0 / (jnp.max(jnp.sum(jnp.abs(m), axis=0)) * 1.00001))

    def column(vector):
        return jnp.broadcast_to(vector[:, None], (N, 128))

    w0 = careful_product(v, column(vector[0]))
    g, w = v, w0
    r0 = lax.dynamic_slice_in_dim(v, lax.axis_index("blk") * HALF, HALF, 1)
    r, gains, kept = r0, [], []
    for tier in range(4):
        s, u = comm(tier, g, jnp.broadcast_to(w[:, 0][None, :], (8, N)))
        if tier == 0:
            s = careful_product(s, process_info)
        g = careful_inverse(5.0 * jnp.eye(N, dtype=F32) - s, jnp.float32(1.0 / 5.001))
        both = careful_product(g, jnp.concatenate([r, column(u[0])], axis=1))
        r, w = both[:, :HALF], both[:, HALF:]
        gains.append(g)
        kept.append(both)

    def down(state, of_tier):
        gain, own = of_tier
        return own + careful_product(gain, state), None

    state, _ = lax.scan(down, kept[3], (jnp.stack(gains[2::-1]), jnp.stack(kept[2::-1])))
    state = careful_product(v, careful_product(process_info, state))
    return (w0[:, 0] + state[:, HALF])[None, :], r0 + state[:, :HALF]


def shards(*args):
    mean, near, far, missed = smoother(*args)

    def again(state):
        mean, cov = careful(*args)
        return mean, cov, jnp.zeros_like(cov), jnp.zeros_like(missed)

    mean, near, far, missed = lax.while_loop(lambda state: state[3][0] > 0.5, again, (mean, near, far, missed))
    return mean, near + far


def solution(mesh):
    placed = (P("leaf", None), P("leaf"), P("leaf"), P("leaf", None), P())
    return jax.shard_map(
        shards,
        mesh=mesh,
        in_specs=placed,
        out_specs=(P("leaf", None), P("leaf", "blk")),
        check_vma=False,
    )
```

```python
import functools

import jax
import jax.numpy as jnp
from jax import lax
from jax.experimental import pallas as pl
from jax.experimental.pallas import tpu as pltpu
from jax.sharding import PartitionSpec as P

F32, BF16 = jnp.float32, jnp.bfloat16
MESH = pl.DeviceIdType.MESH
N = 512
HALF = N // 2
VMEM_SPEC = pl.BlockSpec(memory_space=pltpu.VMEM)
ANY_SPEC = pl.BlockSpec(memory_space=pl.ANY)
SMEM_SPEC = pl.BlockSpec(memory_space=pltpu.SMEM)
LIMIT = 60 * 1024 * 1024
NN = ((1,), (0,))
NT = ((1,), (1,))


def dot(a, b, dims=NN, precision=None):
    return lax.dot_general(a, b, (dims, ((), ())), precision=precision, preferred_element_type=F32)


def split(x):
    high = x.astype(BF16)
    return high, (x - high.astype(F32)).astype(BF16)


def split3(x):
    high = x.astype(BF16)
    rest = x - high.astype(F32)
    middle = rest.astype(BF16)
    return high, middle, (rest - middle.astype(F32)).astype(BF16)


def mm3(a, b, dims=NN):
    return dot(a[0], b[0], dims) + (dot(a[0], b[1], dims) + dot(a[1], b[0], dims))


def mm6(a, b):
    small = dot(a[0], b[2]) + (dot(a[1], b[1]) + dot(a[2], b[0]))
    return dot(a[0], b[0]) + ((dot(a[0], b[1]) + dot(a[1], b[0])) + small)


def eye(rows=N, cols=N, offset=0):
    return (
        lax.broadcasted_iota(jnp.int32, (rows, cols), 0) + offset == lax.broadcasted_iota(jnp.int32, (rows, cols), 1)
    ).astype(F32)


def invert(m_ref, xb, rb, mh, mm, ml, alpha, low, steps):
    m = m_ref[...]
    mh[...], mm[...], ml[...] = split3(m)
    grown = 4.0 / ((1.0 + low) * (1.0 + low))
    xb[...] = ((grown * alpha) * ((1.0 + low) * eye() - alpha * m)).astype(BF16)

    def step(index, low):
        factor = 4.0 / ((1.0 + low) * (1.0 + low))
        rb[...] = ((1.0 + low) * eye() - dot(mh[...], xb[...])).astype(BF16)
        later = factor * low
        scale = jnp.where(index == steps - 1, factor * (2.0 / (1.0 + later)), factor)
        xb[...] = (scale * dot(xb[...], rb[...])).astype(BF16)
        return later

    lax.fori_loop(0, steps, step, jnp.float32(grown * low))


def residual(m_ref, xb, rb, mh, mm):
    m_ref[...] = (eye() - dot(xb[...], mh[...])) - dot(xb[...], mm[...])
    rb[...] = m_ref[...].astype(BF16)


def inverse_rows(m_ref, xb, rb, ml, starts, size):
    def rows_of(ref):
        return jnp.concatenate([ref[pl.ds(pl.multiple_of(start, 16), size), :] for start in starts], axis=0)

    count = len(starts) * size
    x_rows = rows_of(xb)
    t = (rows_of(m_ref) - dot(x_rows, ml[...])) + dot(rows_of(rb), rb[...])
    both = dot(jnp.concatenate(split(t), axis=0), xb[...])
    return x_rows.astype(F32) + (both[:count] + both[count:])


def inverse_whole(m_ref, xb, rb, mh, ml):
    square = dot(rb[...], rb[...])
    rb[...], mh[...] = split((m_ref[...] - dot(xb[...], ml[...])) + square)
    whole = xb[...].astype(F32) + (dot(rb[...], xb[...]) + dot(mh[...], xb[...]))
    return whole, jnp.sum(square * square, keepdims=True)


def mm3_row(values, right):
    high, rest, low = split3(values)
    return dot(high, right) + (dot(rest, right) + dot(low, right))


def flagged(vector, below, missed):
    row = lax.broadcasted_iota(jnp.int32, (8, N), 0)
    return jnp.where(row == 1, below + jnp.where(missed < 4e-7, 0.0, 1.0), jnp.where(row == 0, vector, 0.0))


def place(leaf):
    return leaf // 16, (leaf // 4) % 4, leaf % 4


def group(tier, leaf):
    z, y, x = place(leaf)
    return ((x, 1), (y, 4), (z % 4, 16), (z // 4, 64))[tier]


def ring(leaf, mine, stride, k):
    return leaf - mine * stride + ((mine + k) % 4) * stride


def observe(live_ref, rows_ref, values_ref, pattern_ref, q_ref):
    blocks, wide = pattern_ref.shape
    row_of = lax.broadcasted_iota(jnp.int32, (wide, N), 0)
    widen = (lax.broadcasted_iota(jnp.int32, (wide, N), 1) // (N // wide) == row_of).astype(F32)
    keep = dot(pattern_ref[...].astype(F32), widen)
    keep = jnp.where(lax.broadcasted_iota(jnp.int32, (blocks, N), 0) < live_ref[0], keep, 0.0)
    size = N // blocks
    masked = jnp.concatenate(
        [rows_ref[i * size : (i + 1) * size, :] * keep[i : i + 1, :].astype(BF16) for i in range(blocks)], axis=0
    )
    vector = mm3_row(jnp.broadcast_to(values_ref[...], (8, N)), masked)
    return dot(masked, masked, ((0,), (0,))) + q_ref[...], vector


VECTOR, PHASE_A, PHASE_B, PARTNER = 6, 9, 15, 21
SYM_VECTOR, SYM_GATHER, SYM_PARTNER = 9, 12, 21
SEMS = SYM_PARTNER + 12
BLOCK = N // 4
LAST = 256


def sender(tier, send_sems, recv_sems, sent):
    def remote(src, dst, index, device):
        copy = pltpu.make_async_remote_copy(
            src_ref=src, dst_ref=dst, send_sem=send_sems.at[tier, index], recv_sem=recv_sems.at[tier, index],
            device_id=device, device_id_type=MESH,
        )
        copy.start()
        sent.append(copy)
        return copy

    return remote


def exchange_leaves(send, w_ref, parts, vecs, full, u_ref, send_sems, recv_sems, sent, first_work, second_work):
    leaf, core = lax.axis_index("leaf"), lax.axis_index("blk")
    z, y, x = place(leaf)
    remote = sender(0, send_sems, recv_sems, sent)

    def cols(owner, j):
        return pl.ds(pl.multiple_of((owner + j) % 4 * BLOCK, BLOCK), BLOCK)

    def near(k):
        return ring(leaf, x, 1, k), core

    first = [[], [], []]
    for j in range(3):
        for k in (1, 2, 3):
            owner = (x + k) % 4
            part = cols(owner, j)
            first[j].append(remote(send.at[owner, :, :, part], parts.at[x, :, :, part], 3 * j + k - 1, near(k)))
    parts[x] = send[x]
    first_work()
    vecs[0, x] = w_ref[...]
    vectors = [remote(w_ref, vecs.at[0, x], SYM_VECTOR + k - 1, near(k)) for k in (1, 2, 3)]
    gather, halves = [], []

    def piece(owner, j):
        return full.at[0, 2 * owner + core, :, :, cols(owner, j)]

    def to_partner(k, j):
        part = piece((x + 4 - k) % 4, j)
        halves.append(remote(part, part, SYM_PARTNER + 3 * k + j, (leaf, 1 - core)))

    for j in range(3):
        for copy in first[j]:
            copy.wait_recv()
        at = cols(x, j)
        full[0, 2 * x + core, :, :, at] = (parts[0, :, :, at] + parts[1, :, :, at]) + (parts[2, :, :, at] + parts[3, :, :, at])
        part = piece(x, j)
        gather.append([remote(part, part, SYM_GATHER + 3 * j + k - 1, near(k)) for k in (1, 2, 3)])
        to_partner(0, j)
    second_work()
    for j in range(3):
        for k in (1, 3, 2):
            gather[j][k - 1].wait_recv()
            to_partner(k, j)
    for copy in halves:
        copy.wait_recv()
    for copy in vectors:
        copy.wait_recv()
    u_ref[...] = (vecs[0, 0] + vecs[0, 1]) + (vecs[0, 2] + vecs[0, 3])
    for row in range(4):
        col = (row + 3) % 4
        block = full[0, 2 * col : 2 * col + 2, :, :, row * BLOCK : (row + 1) * BLOCK].reshape(BLOCK, BLOCK)
        full[0, 2 * row : 2 * row + 2, :, :, col * BLOCK : (col + 1) * BLOCK] = block.T.reshape(2, 4, 16, BLOCK)


def exchange(tier, send, w_ref, parts, vecs, full, u_ref, send_sems, recv_sems, sent, first_work, second_work):
    leaf, core = lax.axis_index("leaf"), lax.axis_index("blk")
    z, y, x = place(leaf)
    mine, stride = group(tier, leaf)
    strip = core * 4 + x
    strips = pl.ds(core * 4, 4)
    remote = sender(tier, send_sems, recv_sems, sent)

    def cols(h):
        return pl.ds(h * HALF, HALF)

    def spread(part, start, mine, stride):
        return [remote(part, part, start + k - 1, (ring(leaf, mine, stride, k), core)) for k in (1, 2, 3)]

    def to_partner(h, j, part):
        halves.append(remote(part, part, PARTNER + 4 * h + j, (leaf, 1 - core)))

    first, halves = [[], []], []
    for h in (0, 1):
        for k in (1, 2, 3):
            src = send.at[(mine + k) % 4, :, cols(h)] if tier == 1 else send.at[:, cols(h)]
            device = (ring(leaf, mine, stride, k), core)
            first[h].append(remote(src, parts.at[mine, :, cols(h)], 3 * h + k - 1, device))
    parts[mine] = send[mine] if tier == 1 else send[...]
    first_work()
    vecs[tier, mine] = w_ref[...]
    vectors = [
        remote(w_ref, vecs.at[tier, mine], VECTOR + k - 1, (ring(leaf, mine, stride, k), core)) for k in (1, 2, 3)
    ]
    if tier == 3:
        second_work()
    along = []

    def strip_part(number):
        return full.at[tier, number, :, :, cols(0)]

    def level_part(number):
        return full.at[tier, strips, number, :, cols(1)]

    for h in (0, 1):
        for copy in first[h]:
            copy.wait_recv()
        at = slice(h * HALF, (h + 1) * HALF)
        full[tier, strip, y, :, at] = (parts[0, :, at] + parts[1, :, at]) + (parts[2, :, at] + parts[3, :, at])
        own = full.at[tier, strip, y, :, cols(h)]
        along.append(spread(own, PHASE_A, y, 4) if h == 0 else spread(own, PHASE_A + 3, x, 1))
    for copy in along[0]:
        copy.wait_recv()
    by_x = spread(strip_part(strip), PHASE_B, x, 1)
    for copy in along[1]:
        copy.wait_recv()
    by_y = spread(level_part(y), PHASE_B + 3, y, 4)
    to_partner(0, 0, strip_part(strip))
    to_partner(1, 0, level_part(y))
    if tier < 3:
        second_work()
    for k in (1, 3, 2):
        by_x[k - 1].wait_recv()
        to_partner(0, k, strip_part(core * 4 + (x + 4 - k) % 4))
        by_y[k - 1].wait_recv()
        to_partner(1, k, level_part((y + 4 - k) % 4))
    for copy in halves:
        copy.wait_recv()
    for copy in vectors:
        copy.wait_recv()
    u_ref[...] = (vecs[tier, 0] + vecs[tier, 1]) + (vecs[tier, 2] + vecs[tier, 3])


def smoother_kernel(
    live_ref, rows_ref, values_ref, pattern_ref, q_ref, near_ref, q_out, hh, hl, mean_acc, mean_ref, missed_ref,
    m_ref, xb, rb, mh, mm, ml, gh, gl, vector_ref, r, w, u_ref, full, vecs,
    send0, send1, send2, send3, parts0, parts1, parts2, parts3, send_sems, recv_sems,
):
    leaf, core = lax.axis_index("leaf"), lax.axis_index("blk")
    z, y, x = place(leaf)
    barrier = pltpu.get_barrier_semaphore()
    for tier in range(4):
        mine, stride = group(tier, leaf)
        for k in (1, 2, 3):
            peer = (ring(leaf, mine, stride, k), core)
            pl.semaphore_signal(barrier, inc=1, device_id=peer, device_id_type=MESH)
    pl.semaphore_signal(barrier, inc=1, device_id=(leaf, 1 - core), device_id_type=MESH)

    m, vector_ref[...] = observe(live_ref, rows_ref, values_ref, pattern_ref, q_ref)
    m_ref[...] = m
    bound = jnp.max(jnp.sum(jnp.abs(m), axis=0, keepdims=True)) * 1.00001
    invert(m_ref, xb, rb, mh, mm, ml, 1.0 / bound, 1.0 / 64.0, 4)
    residual(m_ref, xb, rb, mh, mm)
    starts = [i * BLOCK + core * 64 for i in range(4)]
    send0[...] = inverse_rows(m_ref, xb, rb, ml, starts, 64).reshape(4, 4, 16, N)
    pl.semaphore_wait(barrier, 13)

    def leaf_first():
        v, missed = inverse_whole(m_ref, xb, rb, mh, ml)
        gh[...], gl[...] = split(v)
        w[0] = flagged(mm3(split(vector_ref[...]), (gh[...], gl[...])), 0.0, missed)
        mean_acc[...] = w[0]
        m_ref[...] = v
        near_ref[...] = m_ref[:, pl.ds(pl.multiple_of(core * HALF, HALF), HALF)]
        r[...] = near_ref[...]

    def leaf_second():
        hh[...], hl[...] = split(mm3((gh[...], gl[...]), split(q_ref[...])))

    def tier_first(n):
        def work():
            gain, missed = inverse_whole(m_ref, xb, rb, mh, ml)
            gh[...], gl[...] = split(gain)
            u = u_ref[...]
            w[n] = flagged(mm3(split(u), (gh[...], gl[...]), NT), u, missed)

        return work

    def tier_second(n):
        def work():
            r[...] = mm3((gh[...], gl[...]), split(r[...]))
            near_ref[...] += mm3((hh[...], hl[...]), split(r[...]))
            mean_acc[...] += mm3(split(w[n]), (hh[...], hl[...]), NT)
            hh[...], hl[...] = split(mm3((hh[...], hl[...]), (gh[...], gl[...])))

        return work

    sends = (send0, send1, send2, send3)
    parts = (parts0, parts1, parts2, parts3)
    sent = []
    for tier in range(4):
        shared = (sends[tier], w.at[tier], parts[tier], vecs, full, u_ref, send_sems, recv_sems, sent)
        if tier == 0:
            exchange_leaves(*shared, leaf_first, leaf_second)
        else:
            exchange(tier, *shared, tier_first(tier), tier_second(tier))
        total = full[tier].reshape(N, N)
        if tier == 0:
            m_ref[...] = 5.0 * eye() - mm6(split3(total), split3(q_ref[...]))
        else:
            m_ref[...] = 5.0 * eye() - total
        invert(m_ref, xb, rb, mh, mm, ml, 1.0 / 5.001, 0.1999, 2)
        if tier < 3:
            residual(m_ref, xb, rb, mh, mm)
        if tier == 0:
            start = core * HALF + x * 64
            send1[...] = inverse_rows(m_ref, xb, rb, ml, [start], 64).reshape(4, 16, N)
        elif tier < 3:
            start = core * HALF + x * 64 + y * 16
            sends[tier + 1][...] = inverse_rows(m_ref, xb, rb, ml, [start], 16)
    resid = (eye() - dot(mh[...], xb[...])) - (dot(mm[...], xb[...]) + dot(ml[...], xb[...]))
    rb[...] = resid.astype(BF16)
    square = dot(rb[...], rb[...])
    rb[...], mh[...] = split(resid + square)
    missed = jnp.where(jnp.sum(square * square, keepdims=True) < 4e-7, 0.0, 1.0)
    missed_ref[0] = jnp.max(u_ref[1:2, 0:128] + missed)
    q = r[...] + mm3((rb[...], mh[...]), split(r[...]))
    q_high, q_low = split(q)
    q_out[...] = dot(xb[...], q_high) + dot(xb[...], q_low)
    u = u_ref[...]
    u = u + mm3(split(u), (rb[...], mh[...]), NT)
    u_high, u_low = split(u)
    mean_ref[...] = dot(u_high, xb[...], NT) + dot(u_low, xb[...], NT)
    for copy in sent:
        copy.wait_send()


def matrix(rows=N, cols=N, dtype=F32):
    return jax.ShapeDtypeStruct((rows, cols), dtype)


def smoother(obs_rows, obs_values, track_blocks, pattern, process_info):
    def square(dtype):
        return pltpu.VMEM((N, N), dtype)

    vector = pltpu.VMEM((8, N), F32)
    pieces = [(4, 16, N), (16, N), (16, N), (16, N)]
    sends = [(4, 4, 16, N), (4, 16, N), (16, N), (16, N)]
    return pl.pallas_call(
        smoother_kernel,
        out_shape=(
            matrix(N, HALF), matrix(N, HALF), matrix(dtype=BF16), matrix(dtype=BF16), matrix(8), matrix(8),
            jax.ShapeDtypeStruct((1,), F32),
        ),
        in_specs=[SMEM_SPEC] + [VMEM_SPEC] * 4,
        out_specs=(VMEM_SPEC,) * 6 + (SMEM_SPEC,),
        scratch_shapes=[
            square(F32), *[square(BF16)] * 7, vector, pltpu.VMEM((N, HALF), F32), pltpu.VMEM((4, 8, N), F32), vector,
            pltpu.VMEM((4, 8, 4, 16, N), F32), pltpu.VMEM((4, 4, 8, N), F32),
            *[pltpu.VMEM(shape, F32) for shape in sends], *[pltpu.VMEM((4, *shape), F32) for shape in pieces],
            pltpu.SemaphoreType.DMA((4, SEMS)), pltpu.SemaphoreType.DMA((4, SEMS)),
        ],
        compiler_params=pltpu.CompilerParams(vmem_limit_bytes=LIMIT, collective_id=0, has_side_effects=True),
    )(track_blocks, obs_rows, obs_values[None, :], pattern, process_info)


def last_kernel(near_ref, q_ref, hh_ref, hl_ref, mean_acc_ref, mean_ref, cov_out, mean_out):
    h = (hh_ref[...], hl_ref[...])
    cov_out[...] = near_ref[...] + mm3(h, split(q_ref[...]))
    mean = mean_acc_ref[...] + mm3(split(mean_ref[...]), h, NT)
    mean_out[...] = mean[0:1, :]


def last(near, q, hh, hl, mean_acc, mean):
    def rows(cols):
        return pl.BlockSpec((LAST, cols), lambda i: (i, 0))

    def lanes(count):
        return pl.BlockSpec((count, LAST), lambda i: (0, i))

    def whole(count, cols):
        return pl.BlockSpec((count, cols), lambda i: (0, 0))

    return pl.pallas_call(
        last_kernel,
        out_shape=(matrix(N, HALF), matrix(1)),
        grid=(N // LAST,),
        in_specs=[rows(HALF), whole(N, HALF), rows(N), rows(N), lanes(8), whole(8, N)],
        out_specs=(rows(HALF), lanes(1)),
        compiler_params=pltpu.CompilerParams(vmem_limit_bytes=LIMIT),
    )(near, q, hh, hl, mean_acc, mean)


ROWS = 64
DEPTH = 128


def chunk(i, size):
    return pl.ds(pl.multiple_of(i * size, size), size)


def careful_rows(left_ref, right_ref, at):
    def add(j, total):
        piece = dot(left_ref[at, chunk(j, DEPTH)], right_ref[chunk(j, DEPTH), :], precision=lax.Precision.HIGHEST)
        return total + piece

    return lax.fori_loop(0, N // DEPTH, add, jnp.zeros((ROWS, right_ref.shape[1]), F32))


def careful_inverse_kernel(alpha_ref, m_ref, out_ref, resid_ref):
    out_ref[...] = alpha_ref[0] * eye()

    def more(state):
        return jnp.logical_and(state[0] < 80, jnp.logical_not(state[1] < 1e-7))

    def again(state):
        def measure(i, total):
            at = chunk(i, ROWS)
            part = eye(ROWS, N, i * ROWS) - careful_rows(m_ref, out_ref, at)
            resid_ref[at, :] = part
            return total + jnp.sum(part * part)

        total = lax.fori_loop(0, N // ROWS, measure, jnp.float32(0.0))

        def update(i, carry):
            at = chunk(i, ROWS)
            out_ref[at, :] = out_ref[at, :] + careful_rows(out_ref, resid_ref, at)
            return carry

        lax.fori_loop(0, N // ROWS, update, 0)
        return state[0] + 1, total

    lax.while_loop(more, again, (jnp.int32(0), jnp.float32(1e30)))


def careful_inverse(m, alpha):
    return pl.pallas_call(
        careful_inverse_kernel,
        out_shape=matrix(),
        in_specs=[SMEM_SPEC, VMEM_SPEC],
        out_specs=VMEM_SPEC,
        scratch_shapes=[pltpu.VMEM((N, N), F32)],
        compiler_params=pltpu.CompilerParams(vmem_limit_bytes=LIMIT),
    )(jnp.reshape(alpha, (1,)), m)


def careful_product_kernel(left_ref, right_ref, out_ref):
    def work(i, carry):
        at = chunk(i, ROWS)
        out_ref[at, :] = careful_rows(left_ref, right_ref, at)
        return carry

    lax.fori_loop(0, N // ROWS, work, 0)


def careful_product(left, right):
    return pl.pallas_call(
        careful_product_kernel,
        out_shape=matrix(N, right.shape[1]),
        in_specs=[VMEM_SPEC, VMEM_SPEC],
        out_specs=VMEM_SPEC,
        compiler_params=pltpu.CompilerParams(vmem_limit_bytes=LIMIT),
    )(left, right)


def comm_kernel(tier, g_ref, w_ref, s_ref, u_ref, parts, vecs, full, sems, send_sems, local_sem):
    leaf, core = lax.axis_index("leaf"), lax.axis_index("blk")
    z, y, x = place(leaf)
    if tier == 0:
        mine, stride = x, 1
    elif tier == 1:
        mine, stride = y, 4
    elif tier == 2:
        mine, stride = z % 4, 16
    else:
        mine, stride = z // 4, 64
    base = leaf - mine * stride

    def sibling(k):
        return base + ((mine + k) % 4) * stride

    def along_y(k):
        return leaf - y * 4 + ((y + k) % 4) * 4

    def along_x(k):
        return leaf - x + (x + k) % 4

    gather_y = tier >= 2
    peers = [sibling(k) for k in (1, 2, 3)]
    if gather_y:
        peers += [along_y(k) for k in (1, 2, 3)]
    if tier >= 1:
        peers += [along_x(k) for k in (1, 2, 3)]
    barrier = pltpu.get_barrier_semaphore()
    for peer in peers:
        pl.semaphore_signal(barrier, inc=1, device_id=(peer, core), device_id_type=MESH)
    pl.semaphore_signal(barrier, inc=1, device_id=(leaf, 1 - core), device_id_type=MESH)
    pl.semaphore_wait(barrier, len(peers) + 1)

    count = 16 if gather_y else 64
    quarter = N // 8

    def rows(c, x_at, y_at=None):
        start = c * HALF + x_at * quarter
        if y_at is not None:
            return pl.ds(pl.multiple_of(start + y_at * 16, 16), 16)
        return pl.ds(pl.multiple_of(start, quarter), quarter)

    def remote(src, dst, index, device):
        return pltpu.make_async_remote_copy(
            src_ref=src, dst_ref=dst, send_sem=send_sems.at[index], recv_sem=sems.at[index],
            device_id=device, device_id_type=MESH,
        )

    if tier == 0:
        own = rows(core, x)
    elif gather_y:
        own = rows(core, x, y)
    else:
        own = rows(core, x)
    first = []
    for k in (1, 2, 3):
        source = rows(core, (x + k) % 4) if tier == 0 else own
        first.append(remote(g_ref.at[source, :], parts.at[mine], k - 1, (sibling(k), core)))
        first.append(remote(w_ref, vecs.at[mine], 2 + k, (sibling(k), core)))
    for copy in first:
        copy.start()
    keep = pltpu.make_async_copy(g_ref.at[own, :], parts.at[mine], local_sem.at[0])
    keep_vec = pltpu.make_async_copy(w_ref, vecs.at[mine], local_sem.at[1])
    keep.start()
    keep_vec.start()
    keep.wait()
    keep_vec.wait()
    for copy in first:
        copy.wait()
    full[own, :] = (parts[0] + parts[1]) + (parts[2] + parts[3])
    u_ref[...] = (vecs[0] + vecs[1]) + (vecs[2] + vecs[3])
    if gather_y:
        second = [remote(full.at[own, :], full.at[own, :], 5 + k, (along_y(k), core)) for k in (1, 2, 3)]
        for copy in second:
            copy.start()
        for copy in second:
            copy.wait()
    quarter_rows = rows(core, x)
    third = [remote(full.at[quarter_rows, :], full.at[quarter_rows, :], 8 + k, (along_x(k), core)) for k in (1, 2, 3)]
    for copy in third:
        copy.start()
    partner = (leaf, 1 - core)
    last = [remote(full.at[quarter_rows, :], full.at[quarter_rows, :], 12, partner)]
    last[0].start()
    for k in (1, 2, 3):
        third[k - 1].wait_recv()
        arrived = rows(core, (x + 4 - k) % 4)
        copy = remote(full.at[arrived, :], full.at[arrived, :], 12 + k, partner)
        copy.start()
        last.append(copy)
    for copy in third:
        copy.wait_send()
    for copy in last:
        copy.wait()
    s_ref[...] = full[...]


def comm(tier, g, w):
    count = 16 if tier >= 2 else 64
    return pl.pallas_call(
        functools.partial(comm_kernel, tier),
        out_shape=(jax.ShapeDtypeStruct((N, N), F32), jax.ShapeDtypeStruct((8, N), F32)),
        in_specs=[VMEM_SPEC, VMEM_SPEC],
        out_specs=(VMEM_SPEC, VMEM_SPEC),
        scratch_shapes=[
            pltpu.VMEM((4, count, N), F32),
            pltpu.VMEM((4, 8, N), F32),
            pltpu.VMEM((N, N), F32),
            pltpu.SemaphoreType.DMA((16,)),
            pltpu.SemaphoreType.DMA((16,)),
            pltpu.SemaphoreType.DMA((2,)),
        ],
        compiler_params=pltpu.CompilerParams(vmem_limit_bytes=LIMIT, collective_id=tier + 1, has_side_effects=True),
    )(g, w)


def careful_leaf_kernel(live_ref, rows_ref, values_ref, pattern_ref, q_ref, m_ref, vector_ref):
    m_ref[...], vector_ref[...] = observe(live_ref, rows_ref, values_ref, pattern_ref, q_ref)


def careful(obs_rows, obs_values, track_blocks, pattern, process_info):
    m, vector = pl.pallas_call(
        careful_leaf_kernel,
        out_shape=(matrix(), matrix(8)),
        in_specs=[SMEM_SPEC] + [VMEM_SPEC] * 4,
        out_specs=(VMEM_SPEC,) * 2,
        compiler_params=pltpu.CompilerParams(vmem_limit_bytes=LIMIT),
    )(track_blocks, obs_rows, obs_values[None, :], pattern, process_info)
    v = careful_inverse(m, 1.0 / (jnp.max(jnp.sum(jnp.abs(m), axis=0)) * 1.00001))

    def column(vector):
        return jnp.broadcast_to(vector[:, None], (N, 128))

    w0 = careful_product(v, column(vector[0]))
    g, w = v, w0
    r0 = lax.dynamic_slice_in_dim(v, lax.axis_index("blk") * HALF, HALF, 1)
    r, gains, kept = r0, [], []
    for tier in range(4):
        s, u = comm(tier, g, jnp.broadcast_to(w[:, 0][None, :], (8, N)))
        if tier == 0:
            s = careful_product(s, process_info)
        g = careful_inverse(5.0 * jnp.eye(N, dtype=F32) - s, jnp.float32(1.0 / 5.001))
        both = careful_product(g, jnp.concatenate([r, column(u[0])], axis=1))
        r, w = both[:, :HALF], both[:, HALF:]
        gains.append(g)
        kept.append(both)

    def down(state, of_tier):
        gain, own = of_tier
        return own + careful_product(gain, state), None

    state, _ = lax.scan(down, kept[3], (jnp.stack(gains[2::-1]), jnp.stack(kept[2::-1])))
    state = careful_product(v, careful_product(process_info, state))
    return (w0[:, 0] + state[:, HALF])[None, :], r0 + state[:, :HALF]


def shards(*args):
    *pieces, missed = smoother(*args)
    cov, mean = last(*pieces)

    def again(state):
        mean, cov = careful(*args)
        return mean, cov, jnp.zeros_like(missed)

    mean, cov, missed = lax.while_loop(lambda state: state[2][0] > 0.5, again, (mean, cov, missed))
    return mean, cov


def solution(mesh):
    placed = (P("leaf", None), P("leaf"), P("leaf"), P("leaf", None), P())
    return jax.shard_map(
        shards,
        mesh=mesh,
        in_specs=placed,
        out_specs=(P("leaf", None), P("leaf", "blk")),
        check_vma=False,
    )
```

```python
import functools

import jax
import jax.numpy as jnp
from jax import lax
from jax.experimental import pallas as pl
from jax.experimental.pallas import tpu as pltpu
from jax.sharding import PartitionSpec as P

F32, BF16 = jnp.float32, jnp.bfloat16
MESH = pl.DeviceIdType.MESH
N = 512
HALF = N // 2
VMEM_SPEC = pl.BlockSpec(memory_space=pltpu.VMEM)
ANY_SPEC = pl.BlockSpec(memory_space=pl.ANY)
SMEM_SPEC = pl.BlockSpec(memory_space=pltpu.SMEM)
LIMIT = 60 * 1024 * 1024
NN = ((1,), (0,))
NT = ((1,), (1,))


def dot(a, b, dims=NN, precision=None):
    return lax.dot_general(a, b, (dims, ((), ())), precision=precision, preferred_element_type=F32)


def split(x):
    high = x.astype(BF16)
    return high, (x - high.astype(F32)).astype(BF16)


def split3(x):
    high = x.astype(BF16)
    rest = x - high.astype(F32)
    middle = rest.astype(BF16)
    return high, middle, (rest - middle.astype(F32)).astype(BF16)


def mm3(a, b, dims=NN):
    return dot(a[0], b[0], dims) + (dot(a[0], b[1], dims) + dot(a[1], b[0], dims))


def mm6(a, b):
    small = dot(a[0], b[2]) + (dot(a[1], b[1]) + dot(a[2], b[0]))
    return dot(a[0], b[0]) + ((dot(a[0], b[1]) + dot(a[1], b[0])) + small)


def eye(rows=N, cols=N, offset=0):
    return (
        lax.broadcasted_iota(jnp.int32, (rows, cols), 0) + offset == lax.broadcasted_iota(jnp.int32, (rows, cols), 1)
    ).astype(F32)


def invert(m_ref, xb, rb, mh, mm, ml, alpha, low, steps):
    m = m_ref[...]
    mh[...], mm[...], ml[...] = split3(m)
    grown = 4.0 / ((1.0 + low) * (1.0 + low))
    xb[...] = ((grown * alpha) * ((1.0 + low) * eye() - alpha * m)).astype(BF16)

    def step(index, low):
        factor = 4.0 / ((1.0 + low) * (1.0 + low))
        rb[...] = ((1.0 + low) * eye() - dot(mh[...], xb[...])).astype(BF16)
        later = factor * low
        scale = jnp.where(index == steps - 1, factor * (2.0 / (1.0 + later)), factor)
        xb[...] = (scale * dot(xb[...], rb[...])).astype(BF16)
        return later

    lax.fori_loop(0, steps, step, jnp.float32(grown * low))


def residual(m_ref, xb, rb, mh, mm):
    m_ref[...] = (eye() - dot(xb[...], mh[...])) - dot(xb[...], mm[...])
    rb[...] = m_ref[...].astype(BF16)


def inverse_rows(m_ref, xb, rb, ml, starts, size):
    def rows_of(ref):
        return jnp.concatenate([ref[pl.ds(pl.multiple_of(start, 16), size), :] for start in starts], axis=0)

    count = len(starts) * size
    x_rows = rows_of(xb)
    t = (rows_of(m_ref) - dot(x_rows, ml[...])) + dot(rows_of(rb), rb[...])
    both = dot(jnp.concatenate(split(t), axis=0), xb[...])
    return x_rows.astype(F32) + (both[:count] + both[count:])


def inverse_whole(m_ref, xb, rb, mh, ml):
    square = dot(rb[...], rb[...])
    rb[...], mh[...] = split((m_ref[...] - dot(xb[...], ml[...])) + square)
    whole = xb[...].astype(F32) + (dot(rb[...], xb[...]) + dot(mh[...], xb[...]))
    return whole, jnp.sum(square * square, keepdims=True)


def mm3_row(values, right):
    high, rest, low = split3(values)
    return dot(high, right) + (dot(rest, right) + dot(low, right))


def flagged(vector, below, missed):
    row = lax.broadcasted_iota(jnp.int32, (8, N), 0)
    return jnp.where(row == 1, below + jnp.where(missed < 4e-7, 0.0, 1.0), jnp.where(row == 0, vector, 0.0))


def place(leaf):
    return leaf // 16, (leaf // 4) % 4, leaf % 4


def group(tier, leaf):
    z, y, x = place(leaf)
    return ((x, 1), (y, 4), (z % 4, 16), (z // 4, 64))[tier]


def ring(leaf, mine, stride, k):
    return leaf - mine * stride + ((mine + k) % 4) * stride


def observe(live_ref, rows_ref, pattern_ref):
    blocks, wide = pattern_ref.shape
    row_of = lax.broadcasted_iota(jnp.int32, (wide, N), 0)
    widen = (lax.broadcasted_iota(jnp.int32, (wide, N), 1) // (N // wide) == row_of).astype(F32)
    keep = dot(pattern_ref[...].astype(F32), widen)
    keep = jnp.where(lax.broadcasted_iota(jnp.int32, (blocks, N), 0) < live_ref[0], keep, 0.0)
    size = N // blocks
    masked = jnp.concatenate(
        [rows_ref[i * size : (i + 1) * size, :] * keep[i : i + 1, :].astype(BF16) for i in range(blocks)], axis=0
    )
    return masked


VECTOR, PHASE_A, PHASE_B, PARTNER = 6, 9, 15, 21
SYM_VECTOR, SYM_GATHER, SYM_PARTNER = 9, 12, 21
SEMS = SYM_PARTNER + 12
BLOCK = N // 4
LAST = 256


def sender(tier, send_sems, recv_sems, sent):
    def remote(src, dst, index, device):
        copy = pltpu.make_async_remote_copy(
            src_ref=src, dst_ref=dst, send_sem=send_sems.at[tier, index], recv_sem=recv_sems.at[tier, index],
            device_id=device, device_id_type=MESH,
        )
        copy.start()
        sent.append(copy)
        return copy

    return remote


def exchange_leaves(send, w_ref, parts, vecs, full, u_ref, send_sems, recv_sems, sent, first_work, second_work):
    leaf, core = lax.axis_index("leaf"), lax.axis_index("blk")
    z, y, x = place(leaf)
    remote = sender(0, send_sems, recv_sems, sent)

    def cols(owner, j):
        return pl.ds(pl.multiple_of((owner + j) % 4 * BLOCK, BLOCK), BLOCK)

    def near(k):
        return ring(leaf, x, 1, k), core

    first = [[], [], []]
    for j in range(3):
        for k in (2, 1, 3):
            owner = (x + k) % 4
            part = cols(owner, j)
            first[j].append(remote(send.at[owner, :, :, part], parts.at[x, :, :, part], 3 * j + k - 1, near(k)))
    parts[x] = send[x]
    first_work()
    vecs[0, x] = w_ref[...]
    vectors = [remote(w_ref, vecs.at[0, x], SYM_VECTOR + k - 1, near(k)) for k in (1, 2, 3)]
    gather, halves = [], []

    def piece(owner, j):
        return full.at[0, 2 * owner + core, :, :, cols(owner, j)]

    def to_partner(k, j):
        part = piece((x + 4 - k) % 4, j)
        halves.append(remote(part, part, SYM_PARTNER + 3 * k + j, (leaf, 1 - core)))

    for j in range(3):
        for copy in first[j]:
            copy.wait_recv()
        at = cols(x, j)
        full[0, 2 * x + core, :, :, at] = (parts[0, :, :, at] + parts[1, :, :, at]) + (parts[2, :, :, at] + parts[3, :, :, at])
        part = piece(x, j)
        gather.append([remote(part, part, SYM_GATHER + 3 * j + k - 1, near(k)) for k in (1, 2, 3)])
        to_partner(0, j)
    second_work()
    for j in range(3):
        for k in (1, 3, 2):
            gather[j][k - 1].wait_recv()
            to_partner(k, j)
    for copy in halves:
        copy.wait_recv()
    for copy in vectors:
        copy.wait_recv()
    u_ref[...] = (vecs[0, 0] + vecs[0, 1]) + (vecs[0, 2] + vecs[0, 3])
    for row in range(4):
        col = (row + 3) % 4
        block = full[0, 2 * col : 2 * col + 2, :, :, row * BLOCK : (row + 1) * BLOCK].reshape(BLOCK, BLOCK)
        full[0, 2 * row : 2 * row + 2, :, :, col * BLOCK : (col + 1) * BLOCK] = block.T.reshape(2, 4, 16, BLOCK)


def exchange(tier, send, w_ref, parts, vecs, full, u_ref, send_sems, recv_sems, sent, first_work, second_work):
    leaf, core = lax.axis_index("leaf"), lax.axis_index("blk")
    z, y, x = place(leaf)
    mine, stride = group(tier, leaf)
    strip = core * 4 + x
    strips = pl.ds(core * 4, 4)
    remote = sender(tier, send_sems, recv_sems, sent)

    def cols(h):
        return pl.ds(h * HALF, HALF)

    def spread(part, start, mine, stride):
        return [remote(part, part, start + k - 1, (ring(leaf, mine, stride, k), core)) for k in (1, 2, 3)]

    def to_partner(h, j, part):
        halves.append(remote(part, part, PARTNER + 4 * h + j, (leaf, 1 - core)))

    first, halves = [[], []], []
    for h in (0, 1):
        for k in (2, 1, 3):
            src = send.at[(mine + k) % 4, :, cols(h)] if tier == 1 else send.at[:, cols(h)]
            device = (ring(leaf, mine, stride, k), core)
            first[h].append(remote(src, parts.at[mine, :, cols(h)], 3 * h + k - 1, device))
    parts[mine] = send[mine] if tier == 1 else send[...]
    first_work()
    vecs[tier, mine] = w_ref[...]
    vectors = [
        remote(w_ref, vecs.at[tier, mine], VECTOR + k - 1, (ring(leaf, mine, stride, k), core)) for k in (1, 2, 3)
    ]
    if tier == 3:
        second_work()
    along = []

    def strip_part(number):
        return full.at[tier, number, :, :, cols(0)]

    def level_part(number):
        return full.at[tier, strips, number, :, cols(1)]

    for h in (0, 1):
        for copy in first[h]:
            copy.wait_recv()
        at = slice(h * HALF, (h + 1) * HALF)
        full[tier, strip, y, :, at] = (parts[0, :, at] + parts[1, :, at]) + (parts[2, :, at] + parts[3, :, at])
        own = full.at[tier, strip, y, :, cols(h)]
        along.append(spread(own, PHASE_A, y, 4) if h == 0 else spread(own, PHASE_A + 3, x, 1))
    for copy in along[0]:
        copy.wait_recv()
    by_x = spread(strip_part(strip), PHASE_B, x, 1)
    for copy in along[1]:
        copy.wait_recv()
    by_y = spread(level_part(y), PHASE_B + 3, y, 4)
    to_partner(0, 0, strip_part(strip))
    to_partner(1, 0, level_part(y))
    if tier < 3:
        second_work()
    for k in (1, 3, 2):
        by_x[k - 1].wait_recv()
        to_partner(0, k, strip_part(core * 4 + (x + 4 - k) % 4))
        by_y[k - 1].wait_recv()
        to_partner(1, k, level_part((y + 4 - k) % 4))
    for copy in halves:
        copy.wait_recv()
    for copy in vectors:
        copy.wait_recv()
    u_ref[...] = (vecs[tier, 0] + vecs[tier, 1]) + (vecs[tier, 2] + vecs[tier, 3])


def smoother_kernel(
    live_ref, rows_ref, values_ref, pattern_ref, q_hbm, near_ref, q_out, hh, hl, mean_acc, mean_ref, missed_ref,
    m_ref, xb, rb, mh, mm, ml, gh, gl, masked_ref, q_ref, q0, q1, q2, r, w, u_ref, full, vecs,
    send0, send1, send2, send3, parts0, parts1, parts2, parts3, send_sems, recv_sems, local_sem,
):
    leaf, core = lax.axis_index("leaf"), lax.axis_index("blk")
    z, y, x = place(leaf)
    barrier = pltpu.get_barrier_semaphore()
    for tier in range(4):
        mine, stride = group(tier, leaf)
        for k in (1, 2, 3):
            peer = (ring(leaf, mine, stride, k), core)
            pl.semaphore_signal(barrier, inc=1, device_id=peer, device_id_type=MESH)
    pl.semaphore_signal(barrier, inc=1, device_id=(leaf, 1 - core), device_id_type=MESH)

    load_q = pltpu.make_async_copy(q_hbm, q_ref, local_sem)
    load_q.start()
    masked_ref[...] = observe(live_ref, rows_ref, pattern_ref)
    gram = dot(masked_ref[...], masked_ref[...], ((0,), (0,)))
    load_q.wait()
    m = gram + q_ref[...]
    m_ref[...] = m
    bound = jnp.max(jnp.sum(jnp.abs(m), axis=0, keepdims=True)) * 1.00001
    invert(m_ref, xb, rb, mh, mm, ml, 1.0 / bound, 1.0 / 64.0, 4)
    residual(m_ref, xb, rb, mh, mm)
    starts = [i * BLOCK + core * 64 for i in range(4)]
    send0[...] = inverse_rows(m_ref, xb, rb, ml, starts, 64).reshape(4, 4, 16, N)
    pl.semaphore_wait(barrier, 13)

    def leaf_first():
        v, missed = inverse_whole(m_ref, xb, rb, mh, ml)
        gh[...], gl[...] = split(v)
        vector = mm3_row(jnp.broadcast_to(values_ref[...], (8, N)), masked_ref[...])
        w[0] = flagged(mm3(split(vector), (gh[...], gl[...])), 0.0, missed)
        mean_acc[...] = w[0]
        m_ref[...] = v
        near_ref[...] = m_ref[:, pl.ds(pl.multiple_of(core * HALF, HALF), HALF)]
        r[...] = near_ref[...]

    def leaf_second():
        q0[...], q1[...], q2[...] = split3(q_ref[...])
        hh[...], hl[...] = split(mm3((gh[...], gl[...]), (q0[...], q1[...])))

    def tier_first(n):
        def work():
            gain, missed = inverse_whole(m_ref, xb, rb, mh, ml)
            gh[...], gl[...] = split(gain)
            u = u_ref[...]
            w[n] = flagged(mm3(split(u), (gh[...], gl[...]), NT), u, missed)

        return work

    def tier_second(n):
        def work():
            r[...] = mm3((gh[...], gl[...]), split(r[...]))
            near_ref[...] += mm3((hh[...], hl[...]), split(r[...]))
            mean_acc[...] += mm3(split(w[n]), (hh[...], hl[...]), NT)
            hh[...], hl[...] = split(mm3((hh[...], hl[...]), (gh[...], gl[...])))

        return work

    sends = (send0, send1, send2, send3)
    parts = (parts0, parts1, parts2, parts3)
    sent = []
    for tier in range(4):
        shared = (sends[tier], w.at[tier], parts[tier], vecs, full, u_ref, send_sems, recv_sems, sent)
        if tier == 0:
            exchange_leaves(*shared, leaf_first, leaf_second)
        else:
            exchange(tier, *shared, tier_first(tier), tier_second(tier))
        total = full[tier].reshape(N, N)
        if tier == 0:
            m_ref[...] = 5.0 * eye() - mm6(split3(total), (q0[...], q1[...], q2[...]))
        else:
            m_ref[...] = 5.0 * eye() - total
        invert(m_ref, xb, rb, mh, mm, ml, 1.0 / 5.001, 0.1999, 2)
        if tier < 3:
            residual(m_ref, xb, rb, mh, mm)
        if tier == 0:
            start = core * HALF + x * 64
            send1[...] = inverse_rows(m_ref, xb, rb, ml, [start], 64).reshape(4, 16, N)
        elif tier < 3:
            start = core * HALF + x * 64 + y * 16
            sends[tier + 1][...] = inverse_rows(m_ref, xb, rb, ml, [start], 16)
    resid = (eye() - dot(mh[...], xb[...])) - (dot(mm[...], xb[...]) + dot(ml[...], xb[...]))
    rb[...] = resid.astype(BF16)
    square = dot(rb[...], rb[...])
    rb[...], mh[...] = split(resid + square)
    missed = jnp.where(jnp.sum(square * square, keepdims=True) < 4e-7, 0.0, 1.0)
    missed_ref[0] = jnp.max(u_ref[1:2, 0:128] + missed)
    q = r[...] + mm3((rb[...], mh[...]), split(r[...]))
    q_high, q_low = split(q)
    q_out[...] = dot(xb[...], q_high) + dot(xb[...], q_low)
    u = u_ref[...]
    u = u + mm3(split(u), (rb[...], mh[...]), NT)
    u_high, u_low = split(u)
    mean_ref[...] = dot(u_high, xb[...], NT) + dot(u_low, xb[...], NT)
    for copy in sent:
        copy.wait_send()


def matrix(rows=N, cols=N, dtype=F32):
    return jax.ShapeDtypeStruct((rows, cols), dtype)


def smoother(obs_rows, obs_values, track_blocks, pattern, process_info):
    def square(dtype):
        return pltpu.VMEM((N, N), dtype)

    vector = pltpu.VMEM((8, N), F32)
    pieces = [(4, 16, N), (16, N), (16, N), (16, N)]
    sends = [(4, 4, 16, N), (4, 16, N), (16, N), (16, N)]
    return pl.pallas_call(
        smoother_kernel,
        out_shape=(
            matrix(N, HALF), matrix(N, HALF), matrix(dtype=BF16), matrix(dtype=BF16), matrix(8), matrix(8),
            jax.ShapeDtypeStruct((1,), F32),
        ),
        in_specs=[SMEM_SPEC] + [VMEM_SPEC] * 3 + [ANY_SPEC],
        out_specs=(VMEM_SPEC,) * 6 + (SMEM_SPEC,),
        scratch_shapes=[
            square(F32), *[square(BF16)] * 8, square(F32), *[square(BF16)] * 3, pltpu.VMEM((N, HALF), F32), pltpu.VMEM((4, 8, N), F32), vector,
            pltpu.VMEM((4, 8, 4, 16, N), F32), pltpu.VMEM((4, 4, 8, N), F32),
            *[pltpu.VMEM(shape, F32) for shape in sends], *[pltpu.VMEM((4, *shape), F32) for shape in pieces],
            pltpu.SemaphoreType.DMA((4, SEMS)), pltpu.SemaphoreType.DMA((4, SEMS)), pltpu.SemaphoreType.DMA,
        ],
        compiler_params=pltpu.CompilerParams(vmem_limit_bytes=LIMIT, collective_id=0, has_side_effects=True),
    )(track_blocks, obs_rows, obs_values[None, :], pattern, process_info)


def last_kernel(near_ref, q_ref, hh_ref, hl_ref, mean_acc_ref, mean_ref, cov_out, mean_out):
    h = (hh_ref[...], hl_ref[...])
    cov_out[...] = near_ref[...] + mm3(h, split(q_ref[...]))
    mean = mean_acc_ref[...] + mm3(split(mean_ref[...]), h, NT)
    mean_out[...] = mean[0:1, :]


def last(near, q, hh, hl, mean_acc, mean):
    def rows(cols):
        return pl.BlockSpec((LAST, cols), lambda i: (i, 0))

    def lanes(count):
        return pl.BlockSpec((count, LAST), lambda i: (0, i))

    def whole(count, cols):
        return pl.BlockSpec((count, cols), lambda i: (0, 0))

    return pl.pallas_call(
        last_kernel,
        out_shape=(matrix(N, HALF), matrix(1)),
        grid=(N // LAST,),
        in_specs=[rows(HALF), whole(N, HALF), rows(N), rows(N), lanes(8), whole(8, N)],
        out_specs=(rows(HALF), lanes(1)),
        compiler_params=pltpu.CompilerParams(vmem_limit_bytes=LIMIT),
    )(near, q, hh, hl, mean_acc, mean)


ROWS = 64
DEPTH = 128


def chunk(i, size):
    return pl.ds(pl.multiple_of(i * size, size), size)


def careful_rows(left_ref, right_ref, at):
    def add(j, total):
        piece = dot(left_ref[at, chunk(j, DEPTH)], right_ref[chunk(j, DEPTH), :], precision=lax.Precision.HIGHEST)
        return total + piece

    return lax.fori_loop(0, N // DEPTH, add, jnp.zeros((ROWS, right_ref.shape[1]), F32))


def careful_inverse_kernel(alpha_ref, m_ref, out_ref, resid_ref):
    out_ref[...] = alpha_ref[0] * eye()

    def more(state):
        return jnp.logical_and(state[0] < 80, jnp.logical_not(state[1] < 1e-7))

    def again(state):
        def measure(i, total):
            at = chunk(i, ROWS)
            part = eye(ROWS, N, i * ROWS) - careful_rows(m_ref, out_ref, at)
            resid_ref[at, :] = part
            return total + jnp.sum(part * part)

        total = lax.fori_loop(0, N // ROWS, measure, jnp.float32(0.0))

        def update(i, carry):
            at = chunk(i, ROWS)
            out_ref[at, :] = out_ref[at, :] + careful_rows(out_ref, resid_ref, at)
            return carry

        lax.fori_loop(0, N // ROWS, update, 0)
        return state[0] + 1, total

    lax.while_loop(more, again, (jnp.int32(0), jnp.float32(1e30)))


def careful_inverse(m, alpha):
    return pl.pallas_call(
        careful_inverse_kernel,
        out_shape=matrix(),
        in_specs=[SMEM_SPEC, VMEM_SPEC],
        out_specs=VMEM_SPEC,
        scratch_shapes=[pltpu.VMEM((N, N), F32)],
        compiler_params=pltpu.CompilerParams(vmem_limit_bytes=LIMIT),
    )(jnp.reshape(alpha, (1,)), m)


def careful_product_kernel(left_ref, right_ref, out_ref):
    def work(i, carry):
        at = chunk(i, ROWS)
        out_ref[at, :] = careful_rows(left_ref, right_ref, at)
        return carry

    lax.fori_loop(0, N // ROWS, work, 0)


def careful_product(left, right):
    return pl.pallas_call(
        careful_product_kernel,
        out_shape=matrix(N, right.shape[1]),
        in_specs=[VMEM_SPEC, VMEM_SPEC],
        out_specs=VMEM_SPEC,
        compiler_params=pltpu.CompilerParams(vmem_limit_bytes=LIMIT),
    )(left, right)


def comm_kernel(tier, g_ref, w_ref, s_ref, u_ref, parts, vecs, full, sems, send_sems, local_sem):
    leaf, core = lax.axis_index("leaf"), lax.axis_index("blk")
    z, y, x = place(leaf)
    if tier == 0:
        mine, stride = x, 1
    elif tier == 1:
        mine, stride = y, 4
    elif tier == 2:
        mine, stride = z % 4, 16
    else:
        mine, stride = z // 4, 64
    base = leaf - mine * stride

    def sibling(k):
        return base + ((mine + k) % 4) * stride

    def along_y(k):
        return leaf - y * 4 + ((y + k) % 4) * 4

    def along_x(k):
        return leaf - x + (x + k) % 4

    gather_y = tier >= 2
    peers = [sibling(k) for k in (1, 2, 3)]
    if gather_y:
        peers += [along_y(k) for k in (1, 2, 3)]
    if tier >= 1:
        peers += [along_x(k) for k in (1, 2, 3)]
    barrier = pltpu.get_barrier_semaphore()
    for peer in peers:
        pl.semaphore_signal(barrier, inc=1, device_id=(peer, core), device_id_type=MESH)
    pl.semaphore_signal(barrier, inc=1, device_id=(leaf, 1 - core), device_id_type=MESH)
    pl.semaphore_wait(barrier, len(peers) + 1)

    count = 16 if gather_y else 64
    quarter = N // 8

    def rows(c, x_at, y_at=None):
        start = c * HALF + x_at * quarter
        if y_at is not None:
            return pl.ds(pl.multiple_of(start + y_at * 16, 16), 16)
        return pl.ds(pl.multiple_of(start, quarter), quarter)

    def remote(src, dst, index, device):
        return pltpu.make_async_remote_copy(
            src_ref=src, dst_ref=dst, send_sem=send_sems.at[index], recv_sem=sems.at[index],
            device_id=device, device_id_type=MESH,
        )

    if tier == 0:
        own = rows(core, x)
    elif gather_y:
        own = rows(core, x, y)
    else:
        own = rows(core, x)
    first = []
    for k in (1, 2, 3):
        source = rows(core, (x + k) % 4) if tier == 0 else own
        first.append(remote(g_ref.at[source, :], parts.at[mine], k - 1, (sibling(k), core)))
        first.append(remote(w_ref, vecs.at[mine], 2 + k, (sibling(k), core)))
    for copy in first:
        copy.start()
    keep = pltpu.make_async_copy(g_ref.at[own, :], parts.at[mine], local_sem.at[0])
    keep_vec = pltpu.make_async_copy(w_ref, vecs.at[mine], local_sem.at[1])
    keep.start()
    keep_vec.start()
    keep.wait()
    keep_vec.wait()
    for copy in first:
        copy.wait()
    full[own, :] = (parts[0] + parts[1]) + (parts[2] + parts[3])
    u_ref[...] = (vecs[0] + vecs[1]) + (vecs[2] + vecs[3])
    if gather_y:
        second = [remote(full.at[own, :], full.at[own, :], 5 + k, (along_y(k), core)) for k in (1, 2, 3)]
        for copy in second:
            copy.start()
        for copy in second:
            copy.wait()
    quarter_rows = rows(core, x)
    third = [remote(full.at[quarter_rows, :], full.at[quarter_rows, :], 8 + k, (along_x(k), core)) for k in (1, 2, 3)]
    for copy in third:
        copy.start()
    partner = (leaf, 1 - core)
    last = [remote(full.at[quarter_rows, :], full.at[quarter_rows, :], 12, partner)]
    last[0].start()
    for k in (1, 2, 3):
        third[k - 1].wait_recv()
        arrived = rows(core, (x + 4 - k) % 4)
        copy = remote(full.at[arrived, :], full.at[arrived, :], 12 + k, partner)
        copy.start()
        last.append(copy)
    for copy in third:
        copy.wait_send()
    for copy in last:
        copy.wait()
    s_ref[...] = full[...]


def comm(tier, g, w):
    count = 16 if tier >= 2 else 64
    return pl.pallas_call(
        functools.partial(comm_kernel, tier),
        out_shape=(jax.ShapeDtypeStruct((N, N), F32), jax.ShapeDtypeStruct((8, N), F32)),
        in_specs=[VMEM_SPEC, VMEM_SPEC],
        out_specs=(VMEM_SPEC, VMEM_SPEC),
        scratch_shapes=[
            pltpu.VMEM((4, count, N), F32),
            pltpu.VMEM((4, 8, N), F32),
            pltpu.VMEM((N, N), F32),
            pltpu.SemaphoreType.DMA((16,)),
            pltpu.SemaphoreType.DMA((16,)),
            pltpu.SemaphoreType.DMA((2,)),
        ],
        compiler_params=pltpu.CompilerParams(vmem_limit_bytes=LIMIT, collective_id=tier + 1, has_side_effects=True),
    )(g, w)


def careful_leaf_kernel(live_ref, rows_ref, values_ref, pattern_ref, q_ref, m_ref, vector_ref):
    masked = observe(live_ref, rows_ref, pattern_ref)
    vector_ref[...] = mm3_row(jnp.broadcast_to(values_ref[...], (8, N)), masked)
    m_ref[...] = dot(masked, masked, ((0,), (0,))) + q_ref[...]


def careful(obs_rows, obs_values, track_blocks, pattern, process_info):
    m, vector = pl.pallas_call(
        careful_leaf_kernel,
        out_shape=(matrix(), matrix(8)),
        in_specs=[SMEM_SPEC] + [VMEM_SPEC] * 4,
        out_specs=(VMEM_SPEC,) * 2,
        compiler_params=pltpu.CompilerParams(vmem_limit_bytes=LIMIT),
    )(track_blocks, obs_rows, obs_values[None, :], pattern, process_info)
    v = careful_inverse(m, 1.0 / (jnp.max(jnp.sum(jnp.abs(m), axis=0)) * 1.00001))

    def column(vector):
        return jnp.broadcast_to(vector[:, None], (N, 128))

    w0 = careful_product(v, column(vector[0]))
    g, w = v, w0
    r0 = lax.dynamic_slice_in_dim(v, lax.axis_index("blk") * HALF, HALF, 1)
    r, gains, kept = r0, [], []
    for tier in range(4):
        s, u = comm(tier, g, jnp.broadcast_to(w[:, 0][None, :], (8, N)))
        if tier == 0:
            s = careful_product(s, process_info)
        g = careful_inverse(5.0 * jnp.eye(N, dtype=F32) - s, jnp.float32(1.0 / 5.001))
        both = careful_product(g, jnp.concatenate([r, column(u[0])], axis=1))
        r, w = both[:, :HALF], both[:, HALF:]
        gains.append(g)
        kept.append(both)

    def down(state, of_tier):
        gain, own = of_tier
        return own + careful_product(gain, state), None

    state, _ = lax.scan(down, kept[3], (jnp.stack(gains[2::-1]), jnp.stack(kept[2::-1])))
    state = careful_product(v, careful_product(process_info, state))
    return (w0[:, 0] + state[:, HALF])[None, :], r0 + state[:, :HALF]


def shards(*args):
    *pieces, missed = smoother(*args)
    cov, mean = last(*pieces)

    def again(state):
        mean, cov = careful(*args)
        return mean, cov, jnp.zeros_like(missed)

    mean, cov, missed = lax.while_loop(lambda state: state[2][0] > 0.5, again, (mean, cov, missed))
    return mean, cov


def solution(mesh):
    placed = (P("leaf", None), P("leaf"), P("leaf"), P("leaf", None), P())
    return jax.shard_map(
        shards,
        mesh=mesh,
        in_specs=placed,
        out_specs=(P("leaf", None), P("leaf", "blk")),
        check_vma=False,
    )
```
